512 devices in a mesh: dp: 8 (over x, y_lo), tm: 64 (over z, y_hi, core).
Axes of the slice: x: 4, y: 4 (y_hi: 2, y_lo: 2; y = y_hi * 2 + y_lo), z: 16, core: 2. Of those that a mesh axis runs over, the one named last changes fastest.
Arguments:
- features: bfloat16 [8, 8192, 1536], P('dp', 'tm'), may hold values from -8 to 8
- start_noise: bfloat16 [8, 8192, 1536], P('dp', 'tm'), may hold values from -1 to 1
- cotangent: bfloat16 [8, 8192, 1536], P('dp', 'tm'), may hold values from -0.0234375 to 0.0234375
- in_weight: bfloat16 [3072, 1536], P('tm'), may hold values from -0.15625 to 0.15625
- kernel: float32 [31, 1536], replicated, may hold values from -1 to 1
- bn_gain: float32 [1536], replicated, may hold values from 0.25 to 1.75
- bn_shift: float32 [1536], replicated, may hold values from -1 to 1
- ends: int32 [8], replicated, may hold values from 4096 to 8192
Outputs:
- perturbation: float32 [8, 8192, 1536], P('dp', 'tm')
- grad_kernel: float32 [31, 1536], P(None, 'tm')
- grad_norm: float32 [2, 1536], P(None, 'tm')
The draws below stay inside these ranges and needn't reach their ends.
Inputs may be any that keep to these rules, and one draw needn't show every extreme that they name: `ends`: frames at or after an utterance's end are padding.
All inputs are finite; a program needn't handle non-finite values.
Results may differ from the reference program's by a relative error of at most 0.0059.
Values may be sent and summed in bfloat16 or wider, within the bound.
A program may use at most 128 MiB of HBM per device.

```python
import jax
import jax.numpy as jnp
from jax import lax

D = 1536
KSIZE = 31
ASCENT = 2
SEQS = 8
FRAMES = 8192


def draw_features(key, part):
    noise_key = jax.random.fold_in(key, 11)
    shared_key = jax.random.fold_in(key, 12)
    noise = jax.random.normal(noise_key, (SEQS, FRAMES, D), jnp.float32)
    shared = jax.random.normal(shared_key, (SEQS, 1, D), jnp.float32)
    ramp = jnp.arange(SEQS, dtype=jnp.float32) / max(SEQS - 1, 1)
    strength = 0.6 * (1.0 + 2.0 * ramp)
    return jnp.clip(noise + strength[:, None, None] * shared, -8.0, 8.0).astype(jnp.bfloat16)


def plant(drawn, own_key, low, largest):
    shape = drawn.shape
    place = [jax.random.randint(jax.random.fold_in(own_key, axis), (), 0, shape[axis]) for axis in range(len(shape))]
    drawn = drawn.at[tuple(place)].set(low)
    longest = shape.index(max(shape))
    place[longest] = (place[longest] + 1) % shape[longest]
    return drawn.at[tuple(place)].set(largest)


def block_levels(key, extent, split, least, high):
    level, own = 1.0, jax.random.fold_in(key, 6)
    for dim, parts in split:
        heights = jnp.exp(jax.random.uniform(jax.random.fold_in(own, dim), (parts,), jnp.float32, least / len(split), high / len(split)))
        level = level * jnp.repeat(heights, extent[dim] // parts).reshape([-1 if axis == dim else 1 for axis in range(len(extent))])
    return level


def scatter_about(key, shape, width, limit, pieces=(), kind=jnp.bfloat16):
    drawn = width * jax.random.normal(key, shape, jnp.float32)
    if pieces:
        drawn = drawn * block_levels(key, shape, pieces, -0.22, 0.18)
    return jnp.clip(drawn, -limit, limit).astype(kind)


def setup_inputs(seed: int = 0) -> dict:
    splits = jax.random.split(jax.random.key(seed), 9)
    return {
        "features": draw_features(jax.random.fold_in(splits[8], 71), 0),
        "start_noise": jnp.clip(jax.random.uniform(splits[1], (SEQS, FRAMES, D), jnp.float32, -1.0, 1.0) * block_levels(splits[1], (SEQS, FRAMES, D), ((0, 8), (1, 64)), -0.4, 0.0), -1.0, 1.0).astype(jnp.bfloat16),
        "cotangent": scatter_about(splits[2], (SEQS, FRAMES, D), (1.0 / (SEQS * FRAMES) ** 0.5), 0.0234375, ((0, 8), (1, 64))),
        "in_weight": scatter_about(splits[3], (2 * D, D), D ** -0.5, 0.15625, ((0, 64),)),
        "kernel": scatter_about(splits[4], (KSIZE, D), KSIZE ** -0.5, 1.0, (), jnp.float32),
        "bn_gain": jnp.clip(1.0 + 0.15 * jax.random.normal(splits[5], (D,), jnp.float32), 0.25, 1.75),
        "bn_shift": jnp.clip(jax.random.uniform(splits[6], (D,), jnp.float32, -1.0, 1.0), -1.0, 1.0),
        "ends": plant(jax.random.randint(splits[7], (SEQS,), FRAMES // 2, FRAMES + 1), jax.random.fold_in(splits[7], 1), FRAMES // 2, FRAMES).astype(jnp.int32),
    }


noise_scale = 0.5
ascent_rate = 0.5
layer_epsilon = 1e-05
batch_epsilon = 1e-05
ascent_epsilon = 1e-06

def normalize(summed):
    centre = summed - lax.optimization_barrier(jnp.mean(summed, axis=-1, keepdims=True))
    inverse = lax.rsqrt(lax.optimization_barrier(jnp.mean(centre * centre, axis=-1, keepdims=True)) + layer_epsilon)
    return (centre * inverse, inverse)

def conv_forward(padded, kernel, out_length):
    result = jnp.zeros((out_length, padded.shape[1]), jnp.float32)
    for offset in range(kernel.shape[0]):
        result = result + kernel[offset] * padded[offset:offset + out_length].astype(jnp.float32)
    return result

def conv_input_grad(padded, kernel, out_length):
    tap_span = kernel.shape[0] - 1
    result = jnp.zeros((out_length, padded.shape[1]), jnp.float32)
    for offset in range(kernel.shape[0]):
        start_row = tap_span - offset
        result = result + kernel[offset] * padded[start_row:start_row + out_length].astype(jnp.float32)
    return result

def conv_kernel_grad(grad_bf, padded, out_length):
    grad_float = grad_bf.astype(jnp.float32)
    rows_list = []
    for offset in range(padded.shape[0] - out_length + 1):
        rows_list.append(lax.optimization_barrier(jnp.sum(grad_float * padded[offset:offset + out_length].astype(jnp.float32), axis=0)))
    return jnp.stack(rows_list)

def reference(features, start_noise, cotangent, in_weight, kernel, bn_gain, bn_shift, ends):
    half_span = (KSIZE - 1) // 2
    model_width = in_weight.shape[1]
    frame_ids = jnp.arange(FRAMES, dtype=jnp.int32)
    live_frames = (frame_ids[None, :] < ends[:, None]).astype(jnp.float32)
    live_count = jnp.sum(ends).astype(jnp.float32)
    lengths = ends.astype(jnp.float32)
    inputs = features.astype(jnp.float32)
    perturbation = noise_scale * start_noise.astype(jnp.float32) * live_frames[:, :, None]
    grad_kernel = jnp.zeros((KSIZE, model_width), jnp.float32)
    grad_gain = jnp.zeros((model_width,), jnp.float32)
    grad_shift = jnp.zeros((model_width,), jnp.float32)

    def project(summed):
        normed, inverse = normalize(summed)
        hidden = jnp.dot(normed.astype(jnp.bfloat16), in_weight.T, preferred_element_type=jnp.float32)
        return (normed, inverse, hidden)

    def forward_one(packed):
        summed, live_mask = packed
        normed, inverse, hidden = project(summed)
        glu = (hidden[:, :model_width] * jax.nn.sigmoid(hidden[:, model_width:]) * live_mask[:, None]).astype(jnp.bfloat16)
        padded = jnp.pad(glu, ((half_span, half_span), (0, 0)))
        return (glu, conv_forward(padded, kernel, FRAMES))

    def kernel_one(packed):
        grad_seq, glu = packed
        padded = jnp.pad(glu, ((half_span, half_span), (0, 0)))
        return conv_kernel_grad(grad_seq, padded, FRAMES)

    def backward_one(packed):
        summed, live_mask, grad_seq, utter_length = packed
        normed, inverse, hidden = project(summed)
        padded = jnp.pad(grad_seq, ((half_span, half_span), (0, 0)))
        grad_glu = (conv_input_grad(padded, kernel, FRAMES) * live_mask[:, None]).astype(jnp.bfloat16)
        grad_glu = lax.optimization_barrier(grad_glu).astype(jnp.float32)
        value_half = hidden[:, :model_width]
        gate_half = jax.nn.sigmoid(hidden[:, model_width:])
        grad_hidden = jnp.concatenate([grad_glu * gate_half, grad_glu * value_half * gate_half * (1.0 - gate_half)], axis=1).astype(jnp.bfloat16)
        grad_normed = jnp.dot(grad_hidden, in_weight, preferred_element_type=jnp.float32)
        grad_sum = inverse * (grad_normed - lax.optimization_barrier(jnp.mean(grad_normed, axis=-1, keepdims=True)) - normed * lax.optimization_barrier(jnp.mean(grad_normed * normed, axis=-1, keepdims=True)))
        direction = live_mask[:, None] * grad_sum
        square_total = jnp.sum(direction * direction)
        return direction * (ascent_rate * jnp.sqrt(utter_length * model_width) / (jnp.sqrt(square_total) + ascent_epsilon))
    for ascent_step in range(ASCENT):
        summed_all = inputs + perturbation
        glu_all, conv_all = lax.map(forward_one, (summed_all, live_frames))
        weights_live = live_frames[:, :, None]
        batch_mean = lax.optimization_barrier(jnp.sum(weights_live * conv_all, axis=(0, 1))) / live_count
        centred = conv_all - batch_mean
        variance = lax.optimization_barrier(jnp.sum(weights_live * centred * centred, axis=(0, 1))) / live_count
        inv_std = lax.rsqrt(variance + batch_epsilon)
        scaled = centred * inv_std
        pre_act = bn_gain * scaled + bn_shift
        pre_sigmoid = jax.nn.sigmoid(pre_act)
        upstream = weights_live * cotangent.astype(jnp.float32) / ASCENT
        grad_pre = upstream * pre_sigmoid * (1.0 + pre_act * (1.0 - pre_sigmoid))
        shift_sum = lax.optimization_barrier(jnp.sum(grad_pre, axis=(0, 1)))
        gain_sum = lax.optimization_barrier(jnp.sum(grad_pre * scaled, axis=(0, 1)))
        grad_shift = grad_shift + shift_sum
        grad_gain = grad_gain + gain_sum
        grad_conv = (weights_live * inv_std * bn_gain * (grad_pre - (shift_sum + scaled * gain_sum) / live_count)).astype(jnp.bfloat16)
        grad_kernel = grad_kernel + lax.optimization_barrier(jnp.sum(lax.map(kernel_one, (grad_conv, glu_all)), axis=0))
        if ascent_step + 1 < ASCENT:
            perturbation = perturbation + lax.map(backward_one, (summed_all, live_frames, grad_conv, lengths))
    return (perturbation, grad_kernel, jnp.stack([grad_gain, grad_shift]))
```

```python
import jax
import jax.numpy as jnp
from jax import lax
from jax.sharding import PartitionSpec as P

ASCENT = 2

noise_scale = 0.5
ascent_rate = 0.5
layer_epsilon = 1e-05
batch_epsilon = 1e-05
ascent_epsilon = 1e-06


def normalize(summed):
    centre = summed - jnp.mean(summed, axis=-1, keepdims=True)
    inverse = lax.rsqrt(jnp.mean(centre * centre, axis=-1, keepdims=True) + layer_epsilon)
    return (centre * inverse, inverse)


def with_halo(block, half_span):
    count = lax.axis_size("tm")
    before = lax.ppermute(block[-half_span:], "tm", [(i, i + 1) for i in range(count - 1)])
    after = lax.ppermute(block[:half_span], "tm", [(i + 1, i) for i in range(count - 1)])
    return jnp.concatenate([before, block, after], axis=0).astype(jnp.float32)


def conv(padded, kernel, out_length, flip):
    taps = kernel.shape[0]
    result = None
    for offset in range(taps):
        start = taps - 1 - offset if flip else offset
        term = kernel[offset] * padded[start : start + out_length]
        result = term if result is None else result + term
    return result


def tap_grad(grad, padded, taps):
    rows = grad.shape[0]
    return jnp.stack([jnp.sum(grad * padded[j : j + rows], axis=0) for j in range(taps)])


def on_device(features, start_noise, cotangent, in_weight, kernel, bn_gain, bn_shift, ends):
    frame_rows = features.shape[1]
    model_width = features.shape[2]
    tap_count = kernel.shape[0]
    half_span = (tap_count - 1) // 2
    shard_index = lax.axis_index("tm")
    group_index = lax.axis_index("dp")
    utter_end = lax.dynamic_index_in_dim(ends, group_index, 0, keepdims=False)
    live_count = jnp.sum(ends).astype(jnp.float32)
    utter_length = utter_end.astype(jnp.float32)
    frame_ids = shard_index * frame_rows + jnp.arange(frame_rows, dtype=jnp.int32)
    live = (frame_ids < utter_end).astype(jnp.float32)[:, None]
    weight_full = lax.all_gather(in_weight, "tm", axis=0, tiled=True)
    inputs = features[0].astype(jnp.float32)
    perturbation = noise_scale * start_noise[0].astype(jnp.float32) * live
    upstream = live * cotangent[0].astype(jnp.float32) / ASCENT
    everywhere = ("dp", "tm")
    kernel_part = 0.0
    norm_part = 0.0
    for ascent_step in range(ASCENT):
        summed = inputs + perturbation
        normed, inverse = normalize(summed)
        hidden = lax.dot_general(
            normed.astype(jnp.bfloat16),
            weight_full,
            (((1,), (1,)), ((), ())),
            preferred_element_type=jnp.float32,
        )
        value_half = hidden[:, :model_width]
        gate_half = jax.nn.sigmoid(hidden[:, model_width:])
        glu = (value_half * gate_half * live).astype(jnp.bfloat16)
        padded = with_halo(glu, half_span)
        conv_out = conv(padded, kernel, frame_rows, False)
        batch_mean = lax.psum(jnp.sum(live * conv_out, axis=0), everywhere) / live_count
        centred = conv_out - batch_mean
        variance = lax.psum(jnp.sum(live * centred * centred, axis=0), everywhere) / live_count
        inv_std = lax.rsqrt(variance + batch_epsilon)
        scaled = centred * inv_std
        pre_act = bn_gain * scaled + bn_shift
        pre_sigmoid = jax.nn.sigmoid(pre_act)
        grad_pre = upstream * pre_sigmoid * (1.0 + pre_act * (1.0 - pre_sigmoid))
        both = lax.psum(
            jnp.stack([jnp.sum(grad_pre * scaled, axis=0), jnp.sum(grad_pre, axis=0)]), everywhere
        )
        norm_part = norm_part + both
        grad_conv = (
            live * inv_std * bn_gain * (grad_pre - (both[1] + scaled * both[0]) / live_count)
        ).astype(jnp.bfloat16)
        kernel_part = kernel_part + tap_grad(grad_conv.astype(jnp.float32), padded, tap_count)
        if ascent_step + 1 < ASCENT:
            grad_pad = with_halo(grad_conv, half_span)
            grad_glu = (conv(grad_pad, kernel, frame_rows, True) * live).astype(jnp.bfloat16)
            grad_float = grad_glu.astype(jnp.float32)
            grad_hidden = jnp.concatenate(
                [grad_float * gate_half, grad_float * value_half * gate_half * (1.0 - gate_half)],
                axis=1,
            ).astype(jnp.bfloat16)
            grad_normed = jnp.dot(grad_hidden, weight_full, preferred_element_type=jnp.float32)
            direction = (
                live
                * inverse
                * (
                    grad_normed
                    - jnp.mean(grad_normed, axis=-1, keepdims=True)
                    - normed * jnp.mean(grad_normed * normed, axis=-1, keepdims=True)
                )
            )
            square_total = lax.psum(jnp.sum(direction * direction), "tm")
            perturbation = perturbation + direction * (
                ascent_rate
                * jnp.sqrt(utter_length * model_width)
                / (jnp.sqrt(square_total) + ascent_epsilon)
            )
    width = model_width // lax.axis_size("tm")
    by_shard = jnp.transpose(kernel_part.reshape(tap_count, -1, width), (1, 0, 2))
    by_shard = jnp.pad(by_shard.reshape(by_shard.shape[0], -1), ((0, 0), (0, 24)))
    kernel_total = lax.psum_scatter(by_shard.reshape(-1, 6, 128), "tm", scatter_dimension=0)
    kernel_total = lax.psum(kernel_total, "dp").reshape(-1)[: tap_count * width]
    kernel_total = kernel_total.reshape(tap_count, width)
    norm_total = lax.dynamic_slice_in_dim(norm_part, shard_index * width, width, 1)
    return (perturbation[None], kernel_total, norm_total)


def solution(mesh):
    return jax.shard_map(
        on_device,
        mesh=mesh,
        in_specs=(
            P("dp", "tm", None),
            P("dp", "tm", None),
            P("dp", "tm", None),
            P("tm", None),
            P(),
            P(),
            P(),
            P(),
        ),
        out_specs=(P("dp", "tm", None), P(None, "tm"), P(None, "tm")),
        check_vma=False,
    )
```

```python
import jax
import jax.numpy as jnp
from jax import lax
from jax.experimental import pallas as pl
from jax.experimental.pallas import tpu as pltpu
from jax.sharding import PartitionSpec as P

ASCENT = 2

noise_scale = 0.5
ascent_rate = 0.5
layer_epsilon = 1e-05
batch_epsilon = 1e-05
ascent_epsilon = 1e-06


def normalize(summed):
    centre = summed - jnp.mean(summed, axis=-1, keepdims=True)
    inverse = lax.rsqrt(jnp.mean(centre * centre, axis=-1, keepdims=True) + layer_epsilon)
    return (centre * inverse, inverse)


def with_halo(block, half_span):
    count = lax.axis_size("tm")
    before = lax.ppermute(block[-half_span:], "tm", [(i, i + 1) for i in range(count - 1)])
    after = lax.ppermute(block[:half_span], "tm", [(i + 1, i) for i in range(count - 1)])
    return jnp.concatenate([before, block, after], axis=0).astype(jnp.float32)


def place():
    dp, tm = lax.axis_index("dp"), lax.axis_index("tm")
    x, y_lo = dp // 2, lax.rem(dp, 2)
    core, y_hi, z = lax.rem(tm, 2), lax.rem(tm // 2, 2), tm // 4
    return x, y_hi * 2 + y_lo, z, core


def device(x, y, z, core):
    return (x * 2 + lax.rem(y, 2), (z * 2 + y // 2) * 2 + core)


def groups():
    x, y, z, core = place()
    pair = (2, core, lambda i: device(x, y, z, i))
    plane = (16, x * 4 + y, lambda i: device(i // 4, lax.rem(i, 4), z, core))
    column = (16, z, lambda i: device(x, y, i, core))
    quad = (4, (y // 2) * 2 + core, lambda i: device(x, (i // 2) * 2 + lax.rem(y, 2), z, lax.rem(i, 2)))
    return pair, plane, column, quad


def meet(*members):
    barrier = pltpu.get_barrier_semaphore()
    for count, mine, where in members:

        def greet(d, carry):
            pl.semaphore_signal(
                barrier,
                inc=1,
                device_id=where(lax.rem(mine + d, count)),
                device_id_type=pl.DeviceIdType.MESH,
            )
            return carry

        lax.fori_loop(1, count, greet, 0)
    pl.semaphore_wait(barrier, sum(count - 1 for count, _, _ in members))


def exchange(group, source, landing, sems):
    count, mine, where = group

    def copy(d, out):
        peer = lax.rem(mine + d, count)
        slot = mine if out else peer
        return pltpu.make_async_remote_copy(
            src_ref=source(peer),
            dst_ref=landing.at[slot],
            send_sem=sems.at[0, d],
            recv_sem=sems.at[1, slot],
            device_id=where(peer),
            device_id_type=pl.DeviceIdType.MESH,
        )

    def start(d, carry):
        copy(d, True).start()
        return carry

    def finish(d, carry):
        copy(d, False).wait_send()
        copy(d, False).wait_recv()
        return carry

    lax.fori_loop(1, count, start, 0)
    lax.fori_loop(1, count, finish, 0)


def add_up(parts, count):
    total = parts[0]
    for i in range(1, count):
        total = total + parts[i]
    return total


def join_moments(parts, count, sizes, stage):
    half = parts.shape[1] // 2
    total = parts[0, :half]
    spread = parts[0, half:]
    for i in range(1, count):
        total = total + parts[i, :half]
        spread = spread + parts[i, half:]
    mean = total * sizes[stage, 2, 0]
    for i in range(count):
        apart = parts[i, :half] - sizes[stage, 0, i] * mean
        spread = spread + apart * apart * sizes[stage, 1, i]
    return jnp.concatenate([total, spread], axis=0)


def sum_everywhere_kernel(moments, sizes, x_ref, out_ref, b0, b1, b2, b3, sems):
    pair, plane, column, _ = groups()
    meet(pair, plane, column)

    def join(parts, count, stage):
        return join_moments(parts, count, sizes, stage) if moments else add_up(parts, count)

    core = pair[1]
    b0[core] = x_ref[core]
    exchange(pair, lambda peer: x_ref.at[peer], b0, sems.at[0])
    b1[plane[1]] = join(b0, 2, 0)
    exchange(plane, lambda peer: b1.at[plane[1]], b1, sems.at[1])
    b2[column[1]] = join(b1, 16, 1)
    exchange(column, lambda peer: b2.at[column[1]], b2, sems.at[2])
    b3[core] = join(b2, 16, 2)
    exchange(pair, lambda peer: b3.at[core], b3, sems.at[3])
    out_ref[...] = b3[...]


def sum_everywhere(first, second, sizes, moments, number):
    packed = jnp.stack([first.reshape(2, 6, 128), second.reshape(2, 6, 128)], axis=1)
    packed = jnp.pad(packed, ((0, 0), (0, 0), (0, 2), (0, 0))).reshape(2, 16, 128)
    out = pl.pallas_call(
        lambda *refs: sum_everywhere_kernel(moments, *refs),
        out_shape=jax.ShapeDtypeStruct((2, 16, 128), jnp.float32),
        in_specs=[
            pl.BlockSpec(memory_space=pltpu.SMEM),
            pl.BlockSpec(memory_space=pltpu.VMEM),
        ],
        out_specs=pl.BlockSpec(memory_space=pltpu.VMEM),
        scratch_shapes=[
            pltpu.VMEM((2, 16, 128), jnp.float32),
            pltpu.VMEM((16, 16, 128), jnp.float32),
            pltpu.VMEM((16, 16, 128), jnp.float32),
            pltpu.VMEM((2, 16, 128), jnp.float32),
            pltpu.SemaphoreType.DMA((4, 2, 16)),
        ],
        compiler_params=pltpu.CompilerParams(collective_id=number, has_side_effects=True),
    )(sizes, packed)
    out = out.reshape(2, 2, 8, 128)[:, :, :6]
    return out[:, 0].reshape(-1), out[:, 1].reshape(-1)


def group_sizes(ends, frame_rows):
    x, y, z, core = place()
    starts = frame_rows * jnp.arange(64, dtype=jnp.int32)
    live = jnp.clip(ends[:, None] - starts[None, :], 0, frame_rows).astype(jnp.float32)
    live = live.reshape(4, 2, 16, 2, 2).transpose(2, 0, 3, 1, 4).reshape(16, 16, 2)
    here = lax.dynamic_index_in_dim(live, z, 0, keepdims=False)
    pair = lax.dynamic_index_in_dim(here, x * 4 + y, 0, keepdims=False)
    sizes = jnp.stack(
        [jnp.pad(pair, (0, 14)), jnp.sum(here, axis=1), jnp.sum(live, axis=(1, 2))]
    )
    each = jnp.where(sizes > 0, 1.0 / jnp.maximum(sizes, 1.0), 0.0)
    whole = jnp.sum(sizes, axis=1, keepdims=True)
    whole = jnp.broadcast_to(1.0 / jnp.maximum(whole, 1.0), sizes.shape)
    return jnp.stack([sizes, each, whole], axis=1)


def square_sum_kernel(x_ref, out_ref, b0, b1, sems):
    _, _, column, quad = groups()
    meet(column, quad)
    b0[column[1]] = x_ref[...]
    exchange(column, lambda peer: b0.at[column[1]], b0, sems.at[0])
    b1[quad[1]] = add_up(b0, 16)
    exchange(quad, lambda peer: b1.at[quad[1]], b1, sems.at[1])
    out_ref[...] = add_up(b1, 4)


def square_sum(rows, number):
    return pl.pallas_call(
        square_sum_kernel,
        out_shape=jax.ShapeDtypeStruct((8, 128), jnp.float32),
        in_specs=[pl.BlockSpec(memory_space=pltpu.VMEM)],
        out_specs=pl.BlockSpec(memory_space=pltpu.VMEM),
        scratch_shapes=[
            pltpu.VMEM((16, 8, 128), jnp.float32),
            pltpu.VMEM((4, 8, 128), jnp.float32),
            pltpu.SemaphoreType.DMA((2, 2, 16)),
        ],
        compiler_params=pltpu.CompilerParams(collective_id=number, has_side_effects=True),
    )(rows)


def scatter_taps_kernel(x_ref, out_ref, b0, b1, b2, s1, s2, sems):
    pair, plane, column, _ = groups()
    x, y, z, core = place()
    meet(pair, plane, column)
    exchange(pair, lambda peer: x_ref.at[peer], b0, sems.at[0])
    s1[...] = x_ref[core] + b0[1 - core]
    b1[z] = s1[z]
    exchange(column, lambda peer: s1.at[peer], b1, sems.at[1])
    s2[...] = add_up(b1, 16)
    b2[plane[1]] = s2[y // 2]
    exchange(plane, lambda peer: s2.at[lax.rem(peer, 4) // 2], b2, sems.at[2])
    out_ref[...] = add_up(b2, 16)


def scatter_taps(taps, number):
    return pl.pallas_call(
        scatter_taps_kernel,
        out_shape=jax.ShapeDtypeStruct((8, 128), jnp.float32),
        in_specs=[pl.BlockSpec(memory_space=pltpu.VMEM)],
        out_specs=pl.BlockSpec(memory_space=pltpu.VMEM),
        scratch_shapes=[
            pltpu.VMEM((2, 16, 2, 8, 128), jnp.float32),
            pltpu.VMEM((16, 2, 8, 128), jnp.float32),
            pltpu.VMEM((16, 8, 128), jnp.float32),
            pltpu.VMEM((16, 2, 8, 128), jnp.float32),
            pltpu.VMEM((2, 8, 128), jnp.float32),
            pltpu.SemaphoreType.DMA((3, 2, 16)),
        ],
        compiler_params=pltpu.CompilerParams(collective_id=number, has_side_effects=True),
    )(taps)


def conv(padded, kernel, out_length, flip):
    taps = kernel.shape[0]
    result = None
    for offset in range(taps):
        start = taps - 1 - offset if flip else offset
        term = kernel[offset] * padded[start : start + out_length]
        result = term if result is None else result + term
    return result


def tap_grad(grad, padded, taps):
    rows = grad.shape[0]
    return jnp.stack([jnp.sum(grad * padded[j : j + rows], axis=0) for j in range(taps)])


def on_device(features, start_noise, cotangent, in_weight, kernel, bn_gain, bn_shift, ends):
    frame_rows = features.shape[1]
    model_width = features.shape[2]
    tap_count = kernel.shape[0]
    half_span = (tap_count - 1) // 2
    shard_index = lax.axis_index("tm")
    group_index = lax.axis_index("dp")
    utter_end = lax.dynamic_index_in_dim(ends, group_index, 0, keepdims=False)
    live_count = jnp.sum(ends).astype(jnp.float32)
    utter_length = utter_end.astype(jnp.float32)
    frame_ids = shard_index * frame_rows + jnp.arange(frame_rows, dtype=jnp.int32)
    live = (frame_ids < utter_end).astype(jnp.float32)[:, None]
    weight_full = lax.all_gather(in_weight, "tm", axis=0, tiled=True)
    inputs = features[0].astype(jnp.float32)
    perturbation = noise_scale * start_noise[0].astype(jnp.float32) * live
    upstream = live * cotangent[0].astype(jnp.float32) / ASCENT
    sizes = group_sizes(ends, frame_rows)
    kernel_part = 0.0
    norm_part = 0.0
    for ascent_step in range(ASCENT):
        summed = inputs + perturbation
        normed, inverse = normalize(summed)
        hidden = lax.dot_general(
            normed.astype(jnp.bfloat16),
            weight_full,
            (((1,), (1,)), ((), ())),
            preferred_element_type=jnp.float32,
        )
        value_half = hidden[:, :model_width]
        gate_half = jax.nn.sigmoid(hidden[:, model_width:])
        glu = (value_half * gate_half * live).astype(jnp.bfloat16)
        padded = with_halo(glu, half_span)
        conv_out = conv(padded, kernel, frame_rows, False)
        local_sum = jnp.sum(live * conv_out, axis=0)
        apart = conv_out - local_sum / jnp.maximum(jnp.sum(live), 1.0)
        total, spread = sum_everywhere(
            local_sum, jnp.sum(live * apart * apart, axis=0), sizes, True, 1 + 2 * ascent_step
        )
        centred = conv_out - total / live_count
        variance = spread / live_count
        inv_std = lax.rsqrt(variance + batch_epsilon)
        scaled = centred * inv_std
        pre_act = bn_gain * scaled + bn_shift
        pre_sigmoid = jax.nn.sigmoid(pre_act)
        grad_pre = upstream * pre_sigmoid * (1.0 + pre_act * (1.0 - pre_sigmoid))
        both = jnp.stack(
            sum_everywhere(
                jnp.sum(grad_pre * scaled, axis=0),
                jnp.sum(grad_pre, axis=0),
                sizes,
                False,
                2 + 2 * ascent_step,
            )
        )
        norm_part = norm_part + both
        grad_conv = (
            live * inv_std * bn_gain * (grad_pre - (both[1] + scaled * both[0]) / live_count)
        ).astype(jnp.bfloat16)
        kernel_part = kernel_part + tap_grad(grad_conv.astype(jnp.float32), padded, tap_count)
        if ascent_step + 1 < ASCENT:
            grad_pad = with_halo(grad_conv, half_span)
            grad_glu = (conv(grad_pad, kernel, frame_rows, True) * live).astype(jnp.bfloat16)
            grad_float = grad_glu.astype(jnp.float32)
            grad_hidden = jnp.concatenate(
                [grad_float * gate_half, grad_float * value_half * gate_half * (1.0 - gate_half)],
                axis=1,
            ).astype(jnp.bfloat16)
            grad_normed = jnp.dot(grad_hidden, weight_full, preferred_element_type=jnp.float32)
            direction = (
                live
                * inverse
                * (
                    grad_normed
                    - jnp.mean(grad_normed, axis=-1, keepdims=True)
                    - normed * jnp.mean(grad_normed * normed, axis=-1, keepdims=True)
                )
            )
            squares = jnp.sum((direction * direction).reshape(16, 8, 12, 128), axis=(0, 2))
            square_total = jnp.sum(square_sum(squares, 5))
            perturbation = perturbation + direction * (
                ascent_rate
                * jnp.sqrt(utter_length * model_width)
                / (jnp.sqrt(square_total) + ascent_epsilon)
            )
    width = model_width // lax.axis_size("tm")
    by_shard = kernel_part.reshape(tap_count, 16, 2, 2, width).transpose(3, 1, 2, 0, 4)
    by_shard = by_shard.reshape(64, tap_count * width)
    by_shard = jnp.pad(by_shard, ((0, 0), (0, 1024 - tap_count * width)))
    kernel_total = scatter_taps(by_shard.reshape(2, 16, 2, 8, 128), 6).reshape(-1)
    kernel_total = kernel_total[: tap_count * width].reshape(tap_count, width)
    norm_total = lax.dynamic_slice_in_dim(norm_part, shard_index * width, width, 1)
    return (perturbation[None], kernel_total, norm_total)


def solution(mesh):
    return jax.shard_map(
        on_device,
        mesh=mesh,
        in_specs=(
            P("dp", "tm", None),
            P("dp", "tm", None),
            P("dp", "tm", None),
            P("tm", None),
            P(),
            P(),
            P(),
            P(),
        ),
        out_specs=(P("dp", "tm", None), P(None, "tm"), P(None, "tm")),
        check_vma=False,
    )
```

```python
import jax
import jax.numpy as jnp
from jax import lax
from jax.experimental import pallas as pl
from jax.experimental.pallas import tpu as pltpu
from jax.sharding import PartitionSpec as P

ASCENT = 2

noise_scale = 0.5
ascent_rate = 0.5
layer_epsilon = 1e-05
batch_epsilon = 1e-05
ascent_epsilon = 1e-06


def normalize(summed):
    centre = summed - jnp.mean(summed, axis=-1, keepdims=True)
    inverse = lax.rsqrt(jnp.mean(centre * centre, axis=-1, keepdims=True) + layer_epsilon)
    return (centre * inverse, inverse)


def with_halo(block, half_span):
    count = lax.axis_size("tm")
    before = lax.ppermute(block[-half_span:], "tm", [(i, i + 1) for i in range(count - 1)])
    after = lax.ppermute(block[:half_span], "tm", [(i + 1, i) for i in range(count - 1)])
    return jnp.concatenate([before, block, after], axis=0).astype(jnp.float32)


def place():
    dp, tm = lax.axis_index("dp"), lax.axis_index("tm")
    x, y_lo = dp // 2, lax.rem(dp, 2)
    core, y_hi, z = lax.rem(tm, 2), lax.rem(tm // 2, 2), tm // 4
    return x, y_hi * 2 + y_lo, z, core


def device(x, y, z, core):
    return (x * 2 + lax.rem(y, 2), (z * 2 + y // 2) * 2 + core)


def groups():
    x, y, z, core = place()
    pair = (2, core, lambda i: device(x, y, z, i))
    plane = (16, x * 4 + y, lambda i: device(i // 4, lax.rem(i, 4), z, core))
    column = (16, z, lambda i: device(x, y, i, core))
    quad = (4, (y // 2) * 2 + core, lambda i: device(x, (i // 2) * 2 + lax.rem(y, 2), z, lax.rem(i, 2)))
    return pair, plane, column, quad


def meet(*members):
    barrier = pltpu.get_barrier_semaphore()
    for count, mine, where in members:

        def greet(d, carry):
            pl.semaphore_signal(
                barrier,
                inc=1,
                device_id=where(lax.rem(mine + d, count)),
                device_id_type=pl.DeviceIdType.MESH,
            )
            return carry

        lax.fori_loop(1, count, greet, 0)
    pl.semaphore_wait(barrier, sum(count - 1 for count, _, _ in members))


def exchange(group, source, landing, sems):
    count, mine, where = group

    def copy(d, out):
        peer = lax.rem(mine + d, count)
        slot = mine if out else peer
        return pltpu.make_async_remote_copy(
            src_ref=source(peer),
            dst_ref=landing.at[slot],
            send_sem=sems.at[0, d],
            recv_sem=sems.at[1, slot],
            device_id=where(peer),
            device_id_type=pl.DeviceIdType.MESH,
        )

    def start(d, carry):
        copy(d, True).start()
        return carry

    def finish(d, carry):
        copy(d, False).wait_send()
        copy(d, False).wait_recv()
        return carry

    lax.fori_loop(1, count, start, 0)
    lax.fori_loop(1, count, finish, 0)


def add_up(parts, count):
    total = parts[0]
    for i in range(1, count):
        total = total + parts[i]
    return total


def join_moments(parts, count, sizes, stage):
    half = parts.shape[1] // 2
    total = parts[0, :half]
    spread = parts[0, half:]
    for i in range(1, count):
        total = total + parts[i, :half]
        spread = spread + parts[i, half:]
    mean = total * sizes[stage, 2, 0]
    for i in range(count):
        apart = parts[i, :half] - sizes[stage, 0, i] * mean
        spread = spread + apart * apart * sizes[stage, 1, i]
    return jnp.concatenate([total, spread], axis=0)


def sum_everywhere_kernel(moments, sizes, x_ref, out_ref, b0, b1, b2, b3, sems):
    pair, plane, column, _ = groups()
    meet(pair, plane, column)

    def join(parts, count, stage):
        return join_moments(parts, count, sizes, stage) if moments else add_up(parts, count)

    core = pair[1]
    b0[core] = x_ref[core]
    exchange(pair, lambda peer: x_ref.at[peer], b0, sems.at[0])
    b1[plane[1]] = join(b0, 2, 0)
    exchange(plane, lambda peer: b1.at[plane[1]], b1, sems.at[1])
    b2[column[1]] = join(b1, 16, 1)
    exchange(column, lambda peer: b2.at[column[1]], b2, sems.at[2])
    b3[core] = join(b2, 16, 2)
    exchange(pair, lambda peer: b3.at[core], b3, sems.at[3])
    out_ref[...] = b3[...]


def sum_everywhere(first, second, sizes, moments, number):
    packed = jnp.stack([first.reshape(2, 6, 128), second.reshape(2, 6, 128)], axis=1)
    packed = jnp.pad(packed, ((0, 0), (0, 0), (0, 2), (0, 0))).reshape(2, 16, 128)
    out = pl.pallas_call(
        lambda *refs: sum_everywhere_kernel(moments, *refs),
        out_shape=jax.ShapeDtypeStruct((2, 16, 128), jnp.float32),
        in_specs=[
            pl.BlockSpec(memory_space=pltpu.SMEM),
            pl.BlockSpec(memory_space=pltpu.VMEM),
        ],
        out_specs=pl.BlockSpec(memory_space=pltpu.VMEM),
        scratch_shapes=[
            pltpu.VMEM((2, 16, 128), jnp.float32),
            pltpu.VMEM((16, 16, 128), jnp.float32),
            pltpu.VMEM((16, 16, 128), jnp.float32),
            pltpu.VMEM((2, 16, 128), jnp.float32),
            pltpu.SemaphoreType.DMA((4, 2, 16)),
        ],
        compiler_params=pltpu.CompilerParams(collective_id=number, has_side_effects=True),
    )(sizes, packed)
    out = out.reshape(2, 2, 8, 128)[:, :, :6]
    return out[:, 0].reshape(-1), out[:, 1].reshape(-1)


def group_sizes(ends, frame_rows):
    x, y, z, core = place()
    starts = frame_rows * jnp.arange(64, dtype=jnp.int32)
    live = jnp.clip(ends[:, None] - starts[None, :], 0, frame_rows).astype(jnp.float32)
    live = live.reshape(4, 2, 16, 2, 2).transpose(2, 0, 3, 1, 4).reshape(16, 16, 2)
    here = lax.dynamic_index_in_dim(live, z, 0, keepdims=False)
    pair = lax.dynamic_index_in_dim(here, x * 4 + y, 0, keepdims=False)
    sizes = jnp.stack(
        [jnp.pad(pair, (0, 14)), jnp.sum(here, axis=1), jnp.sum(live, axis=(1, 2))]
    )
    each = jnp.where(sizes > 0, 1.0 / jnp.maximum(sizes, 1.0), 0.0)
    whole = jnp.sum(sizes, axis=1, keepdims=True)
    whole = jnp.broadcast_to(1.0 / jnp.maximum(whole, 1.0), sizes.shape)
    return jnp.stack([sizes, each, whole], axis=1)


def square_sum_kernel(x_ref, out_ref, b0, b1, sems):
    _, _, column, quad = groups()
    meet(column, quad)
    b0[column[1]] = x_ref[...]
    exchange(column, lambda peer: b0.at[column[1]], b0, sems.at[0])
    b1[quad[1]] = add_up(b0, 16)
    exchange(quad, lambda peer: b1.at[quad[1]], b1, sems.at[1])
    out_ref[...] = add_up(b1, 4)


def square_sum(rows, number):
    return pl.pallas_call(
        square_sum_kernel,
        out_shape=jax.ShapeDtypeStruct((8, 128), jnp.float32),
        in_specs=[pl.BlockSpec(memory_space=pltpu.VMEM)],
        out_specs=pl.BlockSpec(memory_space=pltpu.VMEM),
        scratch_shapes=[
            pltpu.VMEM((16, 8, 128), jnp.float32),
            pltpu.VMEM((4, 8, 128), jnp.float32),
            pltpu.SemaphoreType.DMA((2, 2, 16)),
        ],
        compiler_params=pltpu.CompilerParams(collective_id=number, has_side_effects=True),
    )(rows)


def scatter_taps_kernel(x_ref, out_ref, b0, b1, b2, s1, s2, sems):
    pair, plane, column, _ = groups()
    x, y, z, core = place()
    meet(pair, plane, column)
    exchange(pair, lambda peer: x_ref.at[peer], b0, sems.at[0])
    s1[...] = x_ref[core] + b0[1 - core]
    b1[z] = s1[z]
    exchange(column, lambda peer: s1.at[peer], b1, sems.at[1])
    s2[...] = add_up(b1, 16)
    b2[plane[1]] = s2[y // 2]
    exchange(plane, lambda peer: s2.at[lax.rem(peer, 4) // 2], b2, sems.at[2])
    out_ref[...] = add_up(b2, 16)


def scatter_taps(taps, number):
    return pl.pallas_call(
        scatter_taps_kernel,
        out_shape=jax.ShapeDtypeStruct((8, 128), jnp.float32),
        in_specs=[pl.BlockSpec(memory_space=pltpu.VMEM)],
        out_specs=pl.BlockSpec(memory_space=pltpu.VMEM),
        scratch_shapes=[
            pltpu.VMEM((2, 16, 2, 8, 128), jnp.float32),
            pltpu.VMEM((16, 2, 8, 128), jnp.float32),
            pltpu.VMEM((16, 8, 128), jnp.float32),
            pltpu.VMEM((16, 2, 8, 128), jnp.float32),
            pltpu.VMEM((2, 8, 128), jnp.float32),
            pltpu.SemaphoreType.DMA((3, 2, 16)),
        ],
        compiler_params=pltpu.CompilerParams(collective_id=number, has_side_effects=True),
    )(taps)


def gather_kernel(x_ref, out, column_sems, ring_sems, core_sems, own_sem):
    x, y, z, core = place()
    pair, _, column, _ = groups()
    along_x = (4, x, lambda i: device(i, y, z, core))
    along_y = (4, y, lambda i: device(x, i, z, core))
    barrier = pltpu.get_barrier_semaphore()
    near = [where(lax.rem(mine + d, 4)) for _, mine, where in (along_x, along_y) for d in (1, 3)]
    for target in near + [pair[2](1 - core)]:
        pl.semaphore_signal(
            barrier, inc=1, device_id=target, device_id_type=pl.DeviceIdType.MESH
        )

    def greet(d, carry):
        pl.semaphore_signal(
            barrier,
            inc=1,
            device_id=column[2](lax.rem(z + d, 16)),
            device_id_type=pl.DeviceIdType.MESH,
        )
        return carry

    lax.fori_loop(1, 16, greet, 0)
    pl.semaphore_wait(barrier, 20)

    def lanes(i):
        return pl.ds(pl.multiple_of(i * 384, 128), 384)

    def rows(i):
        return pl.ds(lax.rem(i, 2) * 3, 3)

    def span(first, half):
        return pl.ds(first, 8) if half is None else pl.ds(first + 4 * half, 4)

    def first_x(i, half=None):
        return out.at[span(0, half), y // 2, core, rows(y), :, lanes(i)]

    def first_y(i, half=None):
        return out.at[span(0, half), i // 2, core, rows(i)]

    def second_y(i, half=None):
        return out.at[span(8, half), i // 2, core, rows(i), :, lanes(x)]

    def second_x(i, half=None):
        return out.at[span(8, half), :, core, :, :, lanes(i)]

    def remote(block, sems, number, target):
        return pltpu.make_async_remote_copy(
            src_ref=block,
            dst_ref=block,
            send_sem=sems.at[0, number],
            recv_sem=sems.at[1, number],
            device_id=target,
            device_id_type=pl.DeviceIdType.MESH,
        )

    def piece(i):
        return out.at[i, y // 2, core, rows(y), :, lanes(x)]

    own = pltpu.make_async_copy(x_ref.at[rows(y), :, lanes(x)], piece(z), own_sem)
    own.start()

    def send(d, carry):
        pltpu.make_async_remote_copy(
            src_ref=x_ref.at[rows(y), :, lanes(x)],
            dst_ref=piece(z),
            send_sem=column_sems.at[0, d],
            recv_sem=column_sems.at[1, z],
            device_id=column[2](lax.rem(z + d, 16)),
            device_id_type=pl.DeviceIdType.MESH,
        ).start()
        return carry

    def take(d, carry):
        peer = lax.rem(z + d, 16)
        copy = pltpu.make_async_remote_copy(
            src_ref=x_ref.at[rows(y), :, lanes(x)],
            dst_ref=piece(peer),
            send_sem=column_sems.at[0, d],
            recv_sem=column_sems.at[1, peer],
            device_id=column[2](peer),
            device_id_type=pl.DeviceIdType.MESH,
        )
        copy.wait_send()
        copy.wait_recv()
        return carry

    lax.fori_loop(1, 16, send, 0)
    own.wait()
    lax.fori_loop(1, 16, take, 0)

    def ring(group, block, base, share=None):
        _, mine, where = group
        right, left, far = (lax.rem(mine + d, 4) for d in (1, 3, 2))
        to_right, to_left = where(right), where(left)
        sends = [
            remote(block(mine), ring_sems, base, to_right),
            remote(block(mine), ring_sems, base + 1, to_left),
            remote(block(left, 0), ring_sems, base + 2, to_right),
            remote(block(right, 1), ring_sems, base + 3, to_left),
        ]
        arrivals = [block(left), block(right), block(far, 0), block(far, 1)]
        shared = []

        def arrive(i):
            remote(arrivals[i], ring_sems, base + i, to_left).wait_recv()
            if share is not None:
                give(arrivals[i], share + 1 + i)

        def give(part, number):
            copy = remote(part, core_sems, number, pair[2](1 - core))
            copy.start()
            shared.append(copy)

        def begin():
            sends[0].start()
            sends[1].start()
            if share is not None:
                give(block(mine), share)

        def middle():
            arrive(0)
            sends[2].start()
            arrive(1)
            sends[3].start()

        def end():
            arrive(2)
            arrive(3)

        def drain():
            for copy in sends + shared:
                copy.wait_send()

        return begin, middle, end, drain

    drains = []
    for pass_rings in (
        (ring(along_x, first_x, 0), ring(along_y, second_y, 4)),
        (ring(along_y, first_y, 8, 0), ring(along_x, second_x, 12, 5)),
    ):
        for step in range(3):
            for parts in pass_rings:
                parts[step]()
        drains += [parts[3] for parts in pass_rings]
    for drain in drains:
        drain()
    other = 1 - core

    def theirs_y(i, half=None):
        return out.at[span(0, half), i // 2, other, rows(i)]

    def theirs_x(i, half=None):
        return out.at[span(8, half), :, other, :, :, lanes(i)]

    for block, mine, base in ((theirs_y, y, 0), (theirs_x, x, 5)):
        right, left, far = (lax.rem(mine + d, 4) for d in (1, 3, 2))
        parts = [block(mine), block(left), block(right), block(far, 0), block(far, 1)]
        for i, part in enumerate(parts):
            remote(part, core_sems, base + i, pair[2](other)).wait_recv()


def gather(weight, number):
    shards = weight.shape[0] // 8
    out = pl.pallas_call(
        gather_kernel,
        out_shape=jax.ShapeDtypeStruct((16, 2, 2, shards, 8, weight.shape[1]), weight.dtype),
        in_specs=[pl.BlockSpec(memory_space=pltpu.VMEM)],
        out_specs=pl.BlockSpec(memory_space=pl.ANY),
        scratch_shapes=[
            pltpu.SemaphoreType.DMA((2, 16)),
            pltpu.SemaphoreType.DMA((2, 16)),
            pltpu.SemaphoreType.DMA((2, 10)),
            pltpu.SemaphoreType.DMA,
        ],
        compiler_params=pltpu.CompilerParams(collective_id=number, has_side_effects=True),
    )(weight.reshape(shards, 8, -1))
    return out.reshape(-1, weight.shape[1])


def conv(padded, kernel, out_length, flip):
    taps = kernel.shape[0]
    result = None
    for offset in range(taps):
        start = taps - 1 - offset if flip else offset
        term = kernel[offset] * padded[start : start + out_length]
        result = term if result is None else result + term
    return result


def tap_grad(grad, padded, taps):
    rows = grad.shape[0]
    return jnp.stack([jnp.sum(grad * padded[j : j + rows], axis=0) for j in range(taps)])


def on_device(features, start_noise, cotangent, in_weight, kernel, bn_gain, bn_shift, ends):
    frame_rows = features.shape[1]
    model_width = features.shape[2]
    tap_count = kernel.shape[0]
    half_span = (tap_count - 1) // 2
    shard_index = lax.axis_index("tm")
    group_index = lax.axis_index("dp")
    utter_end = lax.dynamic_index_in_dim(ends, group_index, 0, keepdims=False)
    live_count = jnp.sum(ends).astype(jnp.float32)
    utter_length = utter_end.astype(jnp.float32)
    frame_ids = shard_index * frame_rows + jnp.arange(frame_rows, dtype=jnp.int32)
    live = (frame_ids < utter_end).astype(jnp.float32)[:, None]
    weight_full = gather(in_weight, 7)
    inputs = features[0].astype(jnp.float32)
    perturbation = noise_scale * start_noise[0].astype(jnp.float32) * live
    upstream = live * cotangent[0].astype(jnp.float32) / ASCENT
    sizes = group_sizes(ends, frame_rows)
    kernel_part = 0.0
    norm_part = 0.0
    for ascent_step in range(ASCENT):
        summed = inputs + perturbation
        normed, inverse = normalize(summed)
        hidden = lax.dot_general(
            normed.astype(jnp.bfloat16),
            weight_full,
            (((1,), (1,)), ((), ())),
            preferred_element_type=jnp.float32,
        )
        value_half = hidden[:, :model_width]
        gate_half = jax.nn.sigmoid(hidden[:, model_width:])
        glu = (value_half * gate_half * live).astype(jnp.bfloat16)
        padded = with_halo(glu, half_span)
        conv_out = conv(padded, kernel, frame_rows, False)
        local_sum = jnp.sum(live * conv_out, axis=0)
        apart = conv_out - local_sum / jnp.maximum(jnp.sum(live), 1.0)
        total, spread = sum_everywhere(
            local_sum, jnp.sum(live * apart * apart, axis=0), sizes, True, 1 + 2 * ascent_step
        )
        centred = conv_out - total / live_count
        variance = spread / live_count
        inv_std = lax.rsqrt(variance + batch_epsilon)
        scaled = centred * inv_std
        pre_act = bn_gain * scaled + bn_shift
        pre_sigmoid = jax.nn.sigmoid(pre_act)
        grad_pre = upstream * pre_sigmoid * (1.0 + pre_act * (1.0 - pre_sigmoid))
        both = jnp.stack(
            sum_everywhere(
                jnp.sum(grad_pre * scaled, axis=0),
                jnp.sum(grad_pre, axis=0),
                sizes,
                False,
                2 + 2 * ascent_step,
            )
        )
        norm_part = norm_part + both
        grad_conv = (
            live * inv_std * bn_gain * (grad_pre - (both[1] + scaled * both[0]) / live_count)
        ).astype(jnp.bfloat16)
        kernel_part = kernel_part + tap_grad(grad_conv.astype(jnp.float32), padded, tap_count)
        if ascent_step + 1 < ASCENT:
            grad_pad = with_halo(grad_conv, half_span)
            grad_glu = (conv(grad_pad, kernel, frame_rows, True) * live).astype(jnp.bfloat16)
            grad_float = grad_glu.astype(jnp.float32)
            grad_hidden = jnp.concatenate(
                [grad_float * gate_half, grad_float * value_half * gate_half * (1.0 - gate_half)],
                axis=1,
            ).astype(jnp.bfloat16)
            grad_normed = jnp.dot(grad_hidden, weight_full, preferred_element_type=jnp.float32)
            direction = (
                live
                * inverse
                * (
                    grad_normed
                    - jnp.mean(grad_normed, axis=-1, keepdims=True)
                    - normed * jnp.mean(grad_normed * normed, axis=-1, keepdims=True)
                )
            )
            squares = jnp.sum((direction * direction).reshape(16, 8, 12, 128), axis=(0, 2))
            square_total = jnp.sum(square_sum(squares, 5))
            perturbation = perturbation + direction * (
                ascent_rate
                * jnp.sqrt(utter_length * model_width)
                / (jnp.sqrt(square_total) + ascent_epsilon)
            )
    width = model_width // lax.axis_size("tm")
    by_shard = kernel_part.reshape(tap_count, 16, 2, 2, width).transpose(3, 1, 2, 0, 4)
    by_shard = by_shard.reshape(64, tap_count * width)
    by_shard = jnp.pad(by_shard, ((0, 0), (0, 1024 - tap_count * width)))
    kernel_total = scatter_taps(by_shard.reshape(2, 16, 2, 8, 128), 6).reshape(-1)
    kernel_total = kernel_total[: tap_count * width].reshape(tap_count, width)
    norm_total = lax.dynamic_slice_in_dim(norm_part, shard_index * width, width, 1)
    return (perturbation[None], kernel_total, norm_total)


def solution(mesh):
    return jax.shard_map(
        on_device,
        mesh=mesh,
        in_specs=(
            P("dp", "tm", None),
            P("dp", "tm", None),
            P("dp", "tm", None),
            P("tm", None),
            P(),
            P(),
            P(),
            P(),
        ),
        out_specs=(P("dp", "tm", None), P(None, "tm"), P(None, "tm")),
        check_vma=False,
    )
```

```python
import jax
import jax.numpy as jnp
from jax import lax
from jax.experimental import pallas as pl
from jax.experimental.pallas import tpu as pltpu
from jax.sharding import PartitionSpec as P

ASCENT = 2

noise_scale = 0.5
ascent_rate = 0.5
layer_epsilon = 1e-05
batch_epsilon = 1e-05
ascent_epsilon = 1e-06


def normalize(summed):
    centre = summed - jnp.mean(summed, axis=-1, keepdims=True)
    inverse = lax.rsqrt(jnp.mean(centre * centre, axis=-1, keepdims=True) + layer_epsilon)
    return (centre * inverse, inverse)


def with_halo(block, half_span):
    count = lax.axis_size("tm")
    before = lax.ppermute(block[-half_span:], "tm", [(i, i + 1) for i in range(count - 1)])
    after = lax.ppermute(block[:half_span], "tm", [(i + 1, i) for i in range(count - 1)])
    return jnp.concatenate([before, block, after], axis=0).astype(jnp.float32)


def place():
    dp, tm = lax.axis_index("dp"), lax.axis_index("tm")
    x, y_lo = dp // 2, lax.rem(dp, 2)
    core, y_hi, z = lax.rem(tm, 2), lax.rem(tm // 2, 2), tm // 4
    return x, y_hi * 2 + y_lo, z, core


def device(x, y, z, core):
    return (x * 2 + lax.rem(y, 2), (z * 2 + y // 2) * 2 + core)


def groups():
    x, y, z, core = place()
    pair = (2, core, lambda i: device(x, y, z, i))
    plane = (16, x * 4 + y, lambda i: device(i // 4, lax.rem(i, 4), z, core))
    column = (16, z, lambda i: device(x, y, i, core))
    quad = (4, (y // 2) * 2 + core, lambda i: device(x, (i // 2) * 2 + lax.rem(y, 2), z, lax.rem(i, 2)))
    return pair, plane, column, quad


def meet(*members):
    barrier = pltpu.get_barrier_semaphore()
    for count, mine, where in members:

        def greet(d, carry):
            pl.semaphore_signal(
                barrier,
                inc=1,
                device_id=where(lax.rem(mine + d, count)),
                device_id_type=pl.DeviceIdType.MESH,
            )
            return carry

        lax.fori_loop(1, count, greet, 0)
    pl.semaphore_wait(barrier, sum(count - 1 for count, _, _ in members))


def exchange(group, source, landing, sems):
    count, mine, where = group

    def copy(d, out):
        peer = lax.rem(mine + d, count)
        slot = mine if out else peer
        return pltpu.make_async_remote_copy(
            src_ref=source(peer),
            dst_ref=landing.at[slot],
            send_sem=sems.at[0, d],
            recv_sem=sems.at[1, slot],
            device_id=where(peer),
            device_id_type=pl.DeviceIdType.MESH,
        )

    def start(d, carry):
        copy(d, True).start()
        return carry

    def finish(d, carry):
        copy(d, False).wait_send()
        copy(d, False).wait_recv()
        return carry

    lax.fori_loop(1, count, start, 0)
    lax.fori_loop(1, count, finish, 0)


def add_up(parts, count):
    total = parts[0]
    for i in range(1, count):
        total = total + parts[i]
    return total


def join_moments(parts, count, sizes, stage):
    half = parts.shape[1] // 2
    total = parts[0, :half]
    spread = parts[0, half:]
    for i in range(1, count):
        total = total + parts[i, :half]
        spread = spread + parts[i, half:]
    mean = total * sizes[stage, 2, 0]
    for i in range(count):
        apart = parts[i, :half] - sizes[stage, 0, i] * mean
        spread = spread + apart * apart * sizes[stage, 1, i]
    return jnp.concatenate([total, spread], axis=0)


def flat_plane():
    x, y, z, core = place()
    return (
        32,
        (x * 4 + y) * 2 + core,
        lambda i: device(i // 8, lax.rem(i // 2, 4), z, lax.rem(i, 2)),
    )


def sum_everywhere(src, b1, b2, b3, sems, join):
    plane, column = flat_plane(), groups()[2]
    me, z = plane[1], column[1]
    b1[me] = src[me]
    exchange(plane, lambda peer: src.at[peer], b1, sems.at[0])
    b2[z] = join(b1, 32, 0)
    exchange(column, lambda peer: b2.at[z], b2, sems.at[1])
    b3[me] = join(b2, 16, 1)
    exchange(plane, lambda peer: b3.at[me], b3, sems.at[2])


def batch_norm_kernel(
    sizes, counts, conv_ref, up_ref, live_ref, padded_ref, gain_ref, shift_ref,
    grad_ref, both_ref, taps_ref,
    scaled_ref, pre_ref, inv_ref, s1, a1, a2, a3, s2, c1, c2, c3, sems1, sems2,
):
    meet(flat_plane(), groups()[2])
    tiles = conv_ref.shape[1] // 128
    rows = conv_ref.shape[0]
    total_live = counts[1]

    def at(i):
        return pl.ds(pl.multiple_of(i * 128, 128), 128)

    def each(body):
        def step(i, carry):
            body(i)
            return carry

        lax.fori_loop(0, tiles, step, 0)

    s1[...] = jnp.zeros(s1.shape, jnp.float32)
    s2[...] = jnp.zeros(s2.shape, jnp.float32)

    def moments(i):
        part, live = conv_ref[:, at(i)], live_ref[...]
        local = jnp.sum(part * live, axis=0, keepdims=True)
        apart = part - local * counts[0]
        s1[i, 0:1] = local
        s1[i, 1:2] = jnp.sum(live * apart * apart, axis=0, keepdims=True)

    each(moments)
    sum_everywhere(s1, a1, a2, a3, sems1, lambda p, n, k: join_moments(p, n, sizes, k))

    def activate(i):
        found = a3[i]
        inv_std = lax.rsqrt(found[1:2] / total_live + batch_epsilon)
        scaled = (conv_ref[:, at(i)] - found[0:1] / total_live) * inv_std
        pre_act = gain_ref[:, at(i)] * scaled + shift_ref[:, at(i)]
        pre_sigmoid = jax.nn.sigmoid(pre_act)
        grad_pre = up_ref[:, at(i)] * pre_sigmoid * (1.0 + pre_act * (1.0 - pre_sigmoid))
        scaled_ref[:, at(i)] = scaled
        pre_ref[:, at(i)] = grad_pre
        inv_ref[:, at(i)] = inv_std
        s2[i, 0:1] = jnp.sum(grad_pre * scaled, axis=0, keepdims=True)
        s2[i, 1:2] = jnp.sum(grad_pre, axis=0, keepdims=True)

    each(activate)
    sum_everywhere(s2, c1, c2, c3, sems2, lambda p, n, k: add_up(p, n))

    def backward(i):
        found = c3[i]
        both_ref[:, at(i)] = found
        scaled, grad_pre = scaled_ref[:, at(i)], pre_ref[:, at(i)]
        grad = (
            live_ref[...]
            * (inv_ref[:, at(i)] * gain_ref[:, at(i)])
            * (grad_pre - (found[1:2] + scaled * found[0:1]) / total_live)
        ).astype(jnp.bfloat16)
        grad_ref[:, at(i)] = grad
        grad = grad.astype(jnp.float32)
        for j in range(31):
            window = padded_ref[pl.ds(j, rows), at(i)]
            taps_ref[pl.ds(j, 1), at(i)] = jnp.sum(grad * window, axis=0, keepdims=True)
        taps_ref[pl.ds(31, 1), at(i)] = jnp.zeros((1, 128), jnp.float32)

    each(backward)


def batch_norm(sizes, counts, conv_out, upstream, live, padded, gain, shift, number):
    rows, width = conv_out.shape
    smem, vmem = pl.BlockSpec(memory_space=pltpu.SMEM), pl.BlockSpec(memory_space=pltpu.VMEM)
    slots = [pltpu.VMEM((n, 2, 128), jnp.float32) for n in (32, 32, 16, 32)]
    return pl.pallas_call(
        batch_norm_kernel,
        out_shape=(
            jax.ShapeDtypeStruct((rows, width), jnp.bfloat16),
            jax.ShapeDtypeStruct((2, width), jnp.float32),
            jax.ShapeDtypeStruct((32, width), jnp.float32),
        ),
        in_specs=[smem, smem] + [vmem] * 6,
        out_specs=(vmem, vmem, vmem),
        scratch_shapes=[
            pltpu.VMEM((rows, width), jnp.float32),
            pltpu.VMEM((rows, width), jnp.float32),
            pltpu.VMEM((1, width), jnp.float32),
        ]
        + slots
        + slots
        + [pltpu.SemaphoreType.DMA((3, 2, 32)), pltpu.SemaphoreType.DMA((3, 2, 32))],
        compiler_params=pltpu.CompilerParams(collective_id=number, has_side_effects=True),
    )(sizes, counts, conv_out, upstream, jnp.broadcast_to(live, (rows, 128)), padded,
      gain[None], shift[None])


def group_sizes(ends, frame_rows):
    _, _, z, _ = place()
    starts = frame_rows * jnp.arange(64, dtype=jnp.int32)
    live = jnp.clip(ends[:, None] - starts[None, :], 0, frame_rows).astype(jnp.float32)
    live = live.reshape(4, 2, 16, 2, 2).transpose(2, 0, 3, 1, 4).reshape(16, 32)
    here = lax.dynamic_index_in_dim(live, z, 0, keepdims=False)
    sizes = jnp.stack([here, jnp.pad(jnp.sum(live, axis=1), (0, 16))])
    each = jnp.where(sizes > 0, 1.0 / jnp.maximum(sizes, 1.0), 0.0)
    whole = jnp.sum(sizes, axis=1, keepdims=True)
    whole = jnp.broadcast_to(1.0 / jnp.maximum(whole, 1.0), sizes.shape)
    return jnp.stack([sizes, each, whole], axis=1)


def square_sum_kernel(x_ref, out_ref, b0, b1, sems):
    _, _, column, quad = groups()
    meet(column, quad)
    b0[column[1]] = x_ref[...]
    exchange(column, lambda peer: b0.at[column[1]], b0, sems.at[0])
    b1[quad[1]] = add_up(b0, 16)
    exchange(quad, lambda peer: b1.at[quad[1]], b1, sems.at[1])
    out_ref[...] = add_up(b1, 4)


def square_sum(rows, number):
    return pl.pallas_call(
        square_sum_kernel,
        out_shape=jax.ShapeDtypeStruct((8, 128), jnp.float32),
        in_specs=[pl.BlockSpec(memory_space=pltpu.VMEM)],
        out_specs=pl.BlockSpec(memory_space=pltpu.VMEM),
        scratch_shapes=[
            pltpu.VMEM((16, 8, 128), jnp.float32),
            pltpu.VMEM((4, 8, 128), jnp.float32),
            pltpu.SemaphoreType.DMA((2, 2, 16)),
        ],
        compiler_params=pltpu.CompilerParams(collective_id=number, has_side_effects=True),
    )(rows)


def scatter_taps_kernel(x_ref, out_ref, b0, b1, b2, s1, s2, sems):
    pair, plane, column, _ = groups()
    x, y, z, core = place()
    meet(pair, plane, column)
    exchange(pair, lambda peer: x_ref.at[peer], b0, sems.at[0])
    s1[...] = x_ref[core] + b0[1 - core]
    b1[z] = s1[z]
    exchange(column, lambda peer: s1.at[peer], b1, sems.at[1])
    s2[...] = add_up(b1, 16)
    b2[plane[1]] = s2[y // 2]
    exchange(plane, lambda peer: s2.at[lax.rem(peer, 4) // 2], b2, sems.at[2])
    out_ref[...] = add_up(b2, 16)


def scatter_taps(taps, number):
    return pl.pallas_call(
        scatter_taps_kernel,
        out_shape=jax.ShapeDtypeStruct((8, 128), jnp.float32),
        in_specs=[pl.BlockSpec(memory_space=pltpu.VMEM)],
        out_specs=pl.BlockSpec(memory_space=pltpu.VMEM),
        scratch_shapes=[
            pltpu.VMEM((2, 16, 2, 8, 128), jnp.float32),
            pltpu.VMEM((16, 2, 8, 128), jnp.float32),
            pltpu.VMEM((16, 8, 128), jnp.float32),
            pltpu.VMEM((16, 2, 8, 128), jnp.float32),
            pltpu.VMEM((2, 8, 128), jnp.float32),
            pltpu.SemaphoreType.DMA((3, 2, 16)),
        ],
        compiler_params=pltpu.CompilerParams(collective_id=number, has_side_effects=True),
    )(taps)


def gather_kernel(x_ref, out, column_sems, ring_sems, core_sems, own_sem):
    x, y, z, core = place()
    pair, _, column, _ = groups()
    along_x = (4, x, lambda i: device(i, y, z, core))
    along_y = (4, y, lambda i: device(x, i, z, core))
    barrier = pltpu.get_barrier_semaphore()
    near = [where(lax.rem(mine + d, 4)) for _, mine, where in (along_x, along_y) for d in (1, 3)]
    for target in near + [pair[2](1 - core)]:
        pl.semaphore_signal(
            barrier, inc=1, device_id=target, device_id_type=pl.DeviceIdType.MESH
        )

    def greet(d, carry):
        pl.semaphore_signal(
            barrier,
            inc=1,
            device_id=column[2](lax.rem(z + d, 16)),
            device_id_type=pl.DeviceIdType.MESH,
        )
        return carry

    lax.fori_loop(1, 16, greet, 0)
    pl.semaphore_wait(barrier, 20)

    def lanes(i):
        return pl.ds(pl.multiple_of(i * 384, 128), 384)

    def rows(i):
        return pl.ds(lax.rem(i, 2) * 3, 3)

    def span(first, half):
        return pl.ds(first, 8) if half is None else pl.ds(first + 4 * half, 4)

    def first_x(i, half=None):
        return out.at[span(0, half), y // 2, core, rows(y), :, lanes(i)]

    def first_y(i, half=None):
        return out.at[span(0, half), i // 2, core, rows(i)]

    def second_y(i, half=None):
        return out.at[span(8, half), i // 2, core, rows(i), :, lanes(x)]

    def second_x(i, half=None):
        return out.at[span(8, half), :, core, :, :, lanes(i)]

    def remote(block, sems, number, target):
        return pltpu.make_async_remote_copy(
            src_ref=block,
            dst_ref=block,
            send_sem=sems.at[0, number],
            recv_sem=sems.at[1, number],
            device_id=target,
            device_id_type=pl.DeviceIdType.MESH,
        )

    def piece(i):
        return out.at[i, y // 2, core, rows(y), :, lanes(x)]

    own = pltpu.make_async_copy(x_ref.at[rows(y), :, lanes(x)], piece(z), own_sem)
    own.start()

    def send(d, carry):
        pltpu.make_async_remote_copy(
            src_ref=x_ref.at[rows(y), :, lanes(x)],
            dst_ref=piece(z),
            send_sem=column_sems.at[0, d],
            recv_sem=column_sems.at[1, z],
            device_id=column[2](lax.rem(z + d, 16)),
            device_id_type=pl.DeviceIdType.MESH,
        ).start()
        return carry

    def take(d, carry):
        peer = lax.rem(z + d, 16)
        copy = pltpu.make_async_remote_copy(
            src_ref=x_ref.at[rows(y), :, lanes(x)],
            dst_ref=piece(peer),
            send_sem=column_sems.at[0, d],
            recv_sem=column_sems.at[1, peer],
            device_id=column[2](peer),
            device_id_type=pl.DeviceIdType.MESH,
        )
        copy.wait_send()
        copy.wait_recv()
        return carry

    lax.fori_loop(1, 16, send, 0)
    own.wait()
    lax.fori_loop(1, 16, take, 0)

    def ring(group, block, base, share=None):
        _, mine, where = group
        right, left, far = (lax.rem(mine + d, 4) for d in (1, 3, 2))
        to_right, to_left = where(right), where(left)
        sends = [
            remote(block(mine), ring_sems, base, to_right),
            remote(block(mine), ring_sems, base + 1, to_left),
            remote(block(left, 0), ring_sems, base + 2, to_right),
            remote(block(right, 1), ring_sems, base + 3, to_left),
        ]
        arrivals = [block(left), block(right), block(far, 0), block(far, 1)]
        shared = []

        def arrive(i):
            remote(arrivals[i], ring_sems, base + i, to_left).wait_recv()
            if share is not None:
                give(arrivals[i], share + 1 + i)

        def give(part, number):
            copy = remote(part, core_sems, number, pair[2](1 - core))
            copy.start()
            shared.append(copy)

        def begin():
            sends[0].start()
            sends[1].start()
            if share is not None:
                give(block(mine), share)

        def middle():
            arrive(0)
            sends[2].start()
            arrive(1)
            sends[3].start()

        def end():
            arrive(2)
            arrive(3)

        def drain():
            for copy in sends + shared:
                copy.wait_send()

        return begin, middle, end, drain

    drains = []
    for pass_rings in (
        (ring(along_x, first_x, 0), ring(along_y, second_y, 4)),
        (ring(along_y, first_y, 8, 0), ring(along_x, second_x, 12, 5)),
    ):
        for step in range(3):
            for parts in pass_rings:
                parts[step]()
        drains += [parts[3] for parts in pass_rings]
    for drain in drains:
        drain()
    other = 1 - core

    def theirs_y(i, half=None):
        return out.at[span(0, half), i // 2, other, rows(i)]

    def theirs_x(i, half=None):
        return out.at[span(8, half), :, other, :, :, lanes(i)]

    for block, mine, base in ((theirs_y, y, 0), (theirs_x, x, 5)):
        right, left, far = (lax.rem(mine + d, 4) for d in (1, 3, 2))
        parts = [block(mine), block(left), block(right), block(far, 0), block(far, 1)]
        for i, part in enumerate(parts):
            remote(part, core_sems, base + i, pair[2](other)).wait_recv()


def gather(weight, number):
    shards = weight.shape[0] // 8
    out = pl.pallas_call(
        gather_kernel,
        out_shape=jax.ShapeDtypeStruct((16, 2, 2, shards, 8, weight.shape[1]), weight.dtype),
        in_specs=[pl.BlockSpec(memory_space=pltpu.VMEM)],
        out_specs=pl.BlockSpec(memory_space=pl.ANY),
        scratch_shapes=[
            pltpu.SemaphoreType.DMA((2, 16)),
            pltpu.SemaphoreType.DMA((2, 16)),
            pltpu.SemaphoreType.DMA((2, 10)),
            pltpu.SemaphoreType.DMA,
        ],
        compiler_params=pltpu.CompilerParams(collective_id=number, has_side_effects=True),
    )(weight.reshape(shards, 8, -1))
    return out.reshape(-1, weight.shape[1])


def conv(padded, kernel, out_length, flip):
    taps = kernel.shape[0]
    result = None
    for offset in range(taps):
        start = taps - 1 - offset if flip else offset
        term = kernel[offset] * padded[start : start + out_length]
        result = term if result is None else result + term
    return result


def on_device(features, start_noise, cotangent, in_weight, kernel, bn_gain, bn_shift, ends):
    frame_rows = features.shape[1]
    model_width = features.shape[2]
    tap_count = kernel.shape[0]
    half_span = (tap_count - 1) // 2
    shard_index = lax.axis_index("tm")
    group_index = lax.axis_index("dp")
    utter_end = lax.dynamic_index_in_dim(ends, group_index, 0, keepdims=False)
    live_count = jnp.sum(ends).astype(jnp.float32)
    utter_length = utter_end.astype(jnp.float32)
    frame_ids = shard_index * frame_rows + jnp.arange(frame_rows, dtype=jnp.int32)
    live = (frame_ids < utter_end).astype(jnp.float32)[:, None]
    weight_full = gather(in_weight, 7)
    inputs = features[0].astype(jnp.float32)
    perturbation = noise_scale * start_noise[0].astype(jnp.float32) * live
    upstream = live * cotangent[0].astype(jnp.float32) / ASCENT
    sizes = group_sizes(ends, frame_rows)
    counts = jnp.stack([1.0 / jnp.maximum(jnp.sum(live), 1.0), live_count])
    kernel_part = 0.0
    norm_part = 0.0
    for ascent_step in range(ASCENT):
        summed = inputs + perturbation
        normed, inverse = normalize(summed)
        hidden = lax.dot_general(
            normed.astype(jnp.bfloat16),
            weight_full,
            (((1,), (1,)), ((), ())),
            preferred_element_type=jnp.float32,
        )
        value_half = hidden[:, :model_width]
        gate_half = jax.nn.sigmoid(hidden[:, model_width:])
        glu = (value_half * gate_half * live).astype(jnp.bfloat16)
        padded = with_halo(glu, half_span)
        conv_out = conv(padded, kernel, frame_rows, False)
        grad_conv, both, taps = batch_norm(
            sizes, counts, conv_out, upstream, live, padded, bn_gain, bn_shift, 1 + ascent_step
        )
        norm_part = norm_part + both
        kernel_part = kernel_part + taps
        if ascent_step + 1 < ASCENT:
            grad_pad = with_halo(grad_conv, half_span)
            grad_glu = (conv(grad_pad, kernel, frame_rows, True) * live).astype(jnp.bfloat16)
            grad_float = grad_glu.astype(jnp.float32)
            grad_hidden = jnp.concatenate(
                [grad_float * gate_half, grad_float * value_half * gate_half * (1.0 - gate_half)],
                axis=1,
            ).astype(jnp.bfloat16)
            grad_normed = jnp.dot(grad_hidden, weight_full, preferred_element_type=jnp.float32)
            direction = (
                live
                * inverse
                * (
                    grad_normed
                    - jnp.mean(grad_normed, axis=-1, keepdims=True)
                    - normed * jnp.mean(grad_normed * normed, axis=-1, keepdims=True)
                )
            )
            squares = jnp.sum((direction * direction).reshape(16, 8, 12, 128), axis=(0, 2))
            square_total = jnp.sum(square_sum(squares, 5))
            perturbation = perturbation + direction * (
                ascent_rate
                * jnp.sqrt(utter_length * model_width)
                / (jnp.sqrt(square_total) + ascent_epsilon)
            )
    width = model_width // lax.axis_size("tm")
    by_shard = kernel_part[:tap_count].reshape(tap_count, 16, 2, 2, width).transpose(3, 1, 2, 0, 4)
    by_shard = by_shard.reshape(64, tap_count * width)
    by_shard = jnp.pad(by_shard, ((0, 0), (0, 1024 - tap_count * width)))
    kernel_total = scatter_taps(by_shard.reshape(2, 16, 2, 8, 128), 6).reshape(-1)
    kernel_total = kernel_total[: tap_count * width].reshape(tap_count, width)
    norm_total = lax.dynamic_slice_in_dim(norm_part, shard_index * width, width, 1)
    return (perturbation[None], kernel_total, norm_total)


def solution(mesh):
    return jax.shard_map(
        on_device,
        mesh=mesh,
        in_specs=(
            P("dp", "tm", None),
            P("dp", "tm", None),
            P("dp", "tm", None),
            P("tm", None),
            P(),
            P(),
            P(),
            P(),
        ),
        out_specs=(P("dp", "tm", None), P(None, "tm"), P(None, "tm")),
        check_vma=False,
    )
```

```python
import jax
import jax.numpy as jnp
from jax import lax
from jax.experimental import pallas as pl
from jax.experimental.pallas import tpu as pltpu
from jax.sharding import PartitionSpec as P

ASCENT = 2

noise_scale = 0.5
ascent_rate = 0.5
layer_epsilon = 1e-05
batch_epsilon = 1e-05
ascent_epsilon = 1e-06


def normalize(summed):
    centre = summed - jnp.mean(summed, axis=-1, keepdims=True)
    inverse = lax.rsqrt(jnp.mean(centre * centre, axis=-1, keepdims=True) + layer_epsilon)
    return (centre * inverse, inverse)


def place():
    dp, tm = lax.axis_index("dp"), lax.axis_index("tm")
    x, y_lo = dp // 2, lax.rem(dp, 2)
    core, y_hi, z = lax.rem(tm, 2), lax.rem(tm // 2, 2), tm // 4
    return x, y_hi * 2 + y_lo, z, core


def device(x, y, z, core):
    return (x * 2 + lax.rem(y, 2), (z * 2 + y // 2) * 2 + core)


def groups():
    x, y, z, core = place()
    pair = (2, core, lambda i: device(x, y, z, i))
    plane = (16, x * 4 + y, lambda i: device(i // 4, lax.rem(i, 4), z, core))
    column = (16, z, lambda i: device(x, y, i, core))
    quad = (4, (y // 2) * 2 + core, lambda i: device(x, (i // 2) * 2 + lax.rem(y, 2), z, lax.rem(i, 2)))
    return pair, plane, column, quad


def meet(*members):
    barrier = pltpu.get_barrier_semaphore()
    for count, mine, where in members:

        def greet(d, carry):
            pl.semaphore_signal(
                barrier,
                inc=1,
                device_id=where(lax.rem(mine + d, count)),
                device_id_type=pl.DeviceIdType.MESH,
            )
            return carry

        lax.fori_loop(1, count, greet, 0)
    pl.semaphore_wait(barrier, sum(count - 1 for count, _, _ in members))


def exchange(group, source, landing, sems):
    count, mine, where = group

    def copy(d, out):
        peer = lax.rem(mine + d, count)
        slot = mine if out else peer
        return pltpu.make_async_remote_copy(
            src_ref=source(peer),
            dst_ref=landing.at[slot],
            send_sem=sems.at[0, d],
            recv_sem=sems.at[1, slot],
            device_id=where(peer),
            device_id_type=pl.DeviceIdType.MESH,
        )

    def start(d, carry):
        copy(d, True).start()
        return carry

    def finish(d, carry):
        copy(d, False).wait_send()
        copy(d, False).wait_recv()
        return carry

    lax.fori_loop(1, count, start, 0)
    lax.fori_loop(1, count, finish, 0)


def add_up(parts, count):
    total = parts[0]
    for i in range(1, count):
        total = total + parts[i]
    return total


def join_moments(parts, count, sizes, stage):
    half = parts.shape[1] // 2
    total = parts[0, :half]
    spread = parts[0, half:]
    for i in range(1, count):
        total = total + parts[i, :half]
        spread = spread + parts[i, half:]
    mean = total * sizes[stage, 2, 0]
    for i in range(count):
        apart = parts[i, :half] - sizes[stage, 0, i] * mean
        spread = spread + apart * apart * sizes[stage, 1, i]
    return jnp.concatenate([total, spread], axis=0)


def flat_plane():
    x, y, z, core = place()
    return (
        32,
        (x * 4 + y) * 2 + core,
        lambda i: device(i // 8, lax.rem(i // 2, 4), z, lax.rem(i, 2)),
    )


def sum_everywhere(src, b1, b2, b3, sems, join):
    plane, column = flat_plane(), groups()[2]
    me, z = plane[1], column[1]
    b1[me] = src[me]
    exchange(plane, lambda peer: src.at[peer], b1, sems.at[0])
    b2[z] = join(b1, 32, 0)
    exchange(column, lambda peer: b2.at[z], b2, sems.at[1])
    b3[me] = join(b2, 16, 1)
    exchange(plane, lambda peer: b3.at[me], b3, sems.at[2])


def neighbours():
    dp, tm = lax.axis_index("dp"), lax.axis_index("tm")
    return (3, 0, lambda i: (dp, lax.rem(tm + 1 + (i - 1) * 62, 64)))


def conv_kernel(
    back, sizes, counts, glu_ref, up_ref, live_ref, kernel_ref, gain_ref, shift_ref,
    both_ref, taps_ref, grad_glu_ref,
    padded, conv_ref, scaled_ref, pre_ref, inv_ref, grad_ref, halo1, halo2,
    s1, a1, a2, a3, s2, c1, c2, c3, sems1, sems2, halo_sems,
):
    meet(flat_plane(), groups()[2], neighbours())
    tm = lax.axis_index("tm")
    rows, width = glu_ref.shape
    total_live = counts[1]
    beside = neighbours()[2]

    def at(i):
        return pl.ds(pl.multiple_of(i * 128, 128), 128)

    def each(body):
        def step(i, carry):
            body(i)
            return carry

        lax.fori_loop(0, width // 128, step, 0)

    def halo_copies(block, halo, base):
        return [
            pltpu.make_async_remote_copy(
                src_ref=block.at[pl.ds((rows - 16) * (1 - side), 16)],
                dst_ref=halo.at[side],
                send_sem=halo_sems.at[0, base + side],
                recv_sem=halo_sems.at[1, base + side],
                device_id=beside(1 + side),
                device_id_type=pl.DeviceIdType.MESH,
            )
            for side in (0, 1)
        ]

    def fill(block, halo):
        first = jnp.where(tm > 0, 1.0, 0.0).astype(jnp.float32)
        last = jnp.where(tm < 63, 1.0, 0.0).astype(jnp.float32)

        def tile(i):
            padded[pl.ds(0, 16), at(i)] = halo[0, :, at(i)].astype(jnp.float32) * first
            padded[pl.ds(16, rows), at(i)] = block[:, at(i)].astype(jnp.float32)
            padded[pl.ds(rows + 16, 16), at(i)] = halo[1, :, at(i)].astype(jnp.float32) * last

        each(tile)

    def convolve(i, start_of):
        total = None
        for j in range(31):
            term = kernel_ref[pl.ds(j, 1), at(i)] * padded[pl.ds(start_of(j), rows), at(i)]
            total = term if total is None else total + term
        return total

    first_halo = halo_copies(glu_ref, halo1, 0)
    for copy in first_halo:
        copy.start()
    s1[...] = jnp.zeros(s1.shape, jnp.float32)
    s2[...] = jnp.zeros(s2.shape, jnp.float32)
    for copy in first_halo:
        copy.wait()
    fill(glu_ref, halo1)

    def moments(i):
        part, live = convolve(i, lambda j: j + 1), live_ref[...]
        conv_ref[:, at(i)] = part
        local = jnp.sum(part * live, axis=0, keepdims=True)
        apart = part - local * counts[0]
        s1[i, 0:1] = local
        s1[i, 1:2] = jnp.sum(live * apart * apart, axis=0, keepdims=True)

    each(moments)
    sum_everywhere(s1, a1, a2, a3, sems1, lambda p, n, k: join_moments(p, n, sizes, k))

    def activate(i):
        found = a3[i]
        inv_std = lax.rsqrt(found[1:2] / total_live + batch_epsilon)
        scaled = (conv_ref[:, at(i)] - found[0:1] / total_live) * inv_std
        pre_act = gain_ref[:, at(i)] * scaled + shift_ref[:, at(i)]
        pre_sigmoid = jax.nn.sigmoid(pre_act)
        grad_pre = up_ref[:, at(i)] * pre_sigmoid * (1.0 + pre_act * (1.0 - pre_sigmoid))
        scaled_ref[:, at(i)] = scaled
        pre_ref[:, at(i)] = grad_pre
        inv_ref[:, at(i)] = inv_std
        s2[i, 0:1] = jnp.sum(grad_pre * scaled, axis=0, keepdims=True)
        s2[i, 1:2] = jnp.sum(grad_pre, axis=0, keepdims=True)

    each(activate)
    sum_everywhere(s2, c1, c2, c3, sems2, lambda p, n, k: add_up(p, n))

    def backward(i):
        found = c3[i]
        both_ref[:, at(i)] = found
        scaled, grad_pre = scaled_ref[:, at(i)], pre_ref[:, at(i)]
        grad = (
            live_ref[...]
            * (inv_ref[:, at(i)] * gain_ref[:, at(i)])
            * (grad_pre - (found[1:2] + scaled * found[0:1]) / total_live)
        )
        grad_ref[:, at(i)] = grad.astype(jnp.bfloat16)

    each(backward)
    if back:
        second_halo = halo_copies(grad_ref, halo2, 2)
        for copy in second_halo:
            copy.start()

    def tap_sums(i):
        grad = grad_ref[:, at(i)].astype(jnp.float32)
        for j in range(31):
            window = padded[pl.ds(j + 1, rows), at(i)]
            taps_ref[pl.ds(j, 1), at(i)] = jnp.sum(grad * window, axis=0, keepdims=True)
        taps_ref[pl.ds(31, 1), at(i)] = jnp.zeros((1, 128), jnp.float32)

    each(tap_sums)
    if back:
        for copy in second_halo:
            copy.wait()
        fill(grad_ref, halo2)

        def input_grad(i):
            part = convolve(i, lambda j: 31 - j) * live_ref[...]
            grad_glu_ref[:, at(i)] = part.astype(jnp.bfloat16)

        each(input_grad)


def conv_step(sizes, counts, glu, upstream, live, kernel, gain, shift, back, number):
    rows, width = glu.shape
    smem, vmem = pl.BlockSpec(memory_space=pltpu.SMEM), pl.BlockSpec(memory_space=pltpu.VMEM)
    slots = [pltpu.VMEM((n, 2, 128), jnp.float32) for n in (32, 32, 16, 32)]
    whole = pltpu.VMEM((rows, width), jnp.float32)
    halo = pltpu.VMEM((2, 16, width), jnp.bfloat16)
    shapes = [
        jax.ShapeDtypeStruct((2, width), jnp.float32),
        jax.ShapeDtypeStruct((32, width), jnp.float32),
    ]
    if back:
        shapes.append(jax.ShapeDtypeStruct((rows, width), jnp.bfloat16))

    def body(*refs):
        refs = list(refs) if back else list(refs[:10]) + [None] + list(refs[10:])
        conv_kernel(back, *refs)

    return pl.pallas_call(
        body,
        out_shape=shapes,
        in_specs=[smem, smem] + [vmem] * 6,
        out_specs=[vmem] * len(shapes),
        scratch_shapes=[
            pltpu.VMEM((rows + 32, width), jnp.float32),
            whole,
            whole,
            whole,
            pltpu.VMEM((1, width), jnp.float32),
            pltpu.VMEM((rows, width), jnp.bfloat16),
            halo,
            halo,
        ]
        + slots
        + slots
        + [pltpu.SemaphoreType.DMA((3, 2, 32)), pltpu.SemaphoreType.DMA((3, 2, 32))]
        + [pltpu.SemaphoreType.DMA((2, 4))],
        compiler_params=pltpu.CompilerParams(collective_id=number, has_side_effects=True),
    )(sizes, counts, glu, upstream, jnp.broadcast_to(live, (rows, 128)),
      jnp.pad(kernel, ((0, 1), (0, 0))), gain[None], shift[None])


def group_sizes(ends, frame_rows):
    _, _, z, _ = place()
    starts = frame_rows * jnp.arange(64, dtype=jnp.int32)
    live = jnp.clip(ends[:, None] - starts[None, :], 0, frame_rows).astype(jnp.float32)
    live = live.reshape(4, 2, 16, 2, 2).transpose(2, 0, 3, 1, 4).reshape(16, 32)
    here = lax.dynamic_index_in_dim(live, z, 0, keepdims=False)
    sizes = jnp.stack([here, jnp.pad(jnp.sum(live, axis=1), (0, 16))])
    each = jnp.where(sizes > 0, 1.0 / jnp.maximum(sizes, 1.0), 0.0)
    whole = jnp.sum(sizes, axis=1, keepdims=True)
    whole = jnp.broadcast_to(1.0 / jnp.maximum(whole, 1.0), sizes.shape)
    return jnp.stack([sizes, each, whole], axis=1)


def square_sum_kernel(x_ref, out_ref, b0, b1, sems):
    _, _, column, quad = groups()
    meet(column, quad)
    b0[column[1]] = x_ref[...]
    exchange(column, lambda peer: b0.at[column[1]], b0, sems.at[0])
    b1[quad[1]] = add_up(b0, 16)
    exchange(quad, lambda peer: b1.at[quad[1]], b1, sems.at[1])
    out_ref[...] = add_up(b1, 4)


def square_sum(rows, number):
    return pl.pallas_call(
        square_sum_kernel,
        out_shape=jax.ShapeDtypeStruct((1, 128), jnp.float32),
        in_specs=[pl.BlockSpec(memory_space=pltpu.VMEM)],
        out_specs=pl.BlockSpec(memory_space=pltpu.VMEM),
        scratch_shapes=[
            pltpu.VMEM((16, 1, 128), jnp.float32),
            pltpu.VMEM((4, 1, 128), jnp.float32),
            pltpu.SemaphoreType.DMA((2, 2, 16)),
        ],
        compiler_params=pltpu.CompilerParams(collective_id=number, has_side_effects=True),
    )(rows)


def scatter_taps_kernel(x_ref, out_ref, b0, b1, b2, s1, s2, sems):
    pair, plane, column, _ = groups()
    x, y, z, core = place()
    meet(pair, plane, column)
    exchange(pair, lambda peer: x_ref.at[peer], b0, sems.at[0])
    s1[...] = x_ref[core] + b0[1 - core]
    b1[z] = s1[z]
    exchange(column, lambda peer: s1.at[peer], b1, sems.at[1])
    s2[...] = add_up(b1, 16)
    b2[plane[1]] = s2[y // 2]
    exchange(plane, lambda peer: s2.at[lax.rem(peer, 4) // 2], b2, sems.at[2])
    out_ref[...] = add_up(b2, 16)


def scatter_taps(taps, number):
    return pl.pallas_call(
        scatter_taps_kernel,
        out_shape=jax.ShapeDtypeStruct((8, 128), jnp.float32),
        in_specs=[pl.BlockSpec(memory_space=pltpu.VMEM)],
        out_specs=pl.BlockSpec(memory_space=pltpu.VMEM),
        scratch_shapes=[
            pltpu.VMEM((2, 16, 2, 8, 128), jnp.float32),
            pltpu.VMEM((16, 2, 8, 128), jnp.float32),
            pltpu.VMEM((16, 8, 128), jnp.float32),
            pltpu.VMEM((16, 2, 8, 128), jnp.float32),
            pltpu.VMEM((2, 8, 128), jnp.float32),
            pltpu.SemaphoreType.DMA((3, 2, 16)),
        ],
        compiler_params=pltpu.CompilerParams(collective_id=number, has_side_effects=True),
    )(taps)


def gather_kernel(x_ref, out, column_sems, ring_sems, core_sems, own_sem):
    x, y, z, core = place()
    pair, _, column, _ = groups()
    along_x = (4, x, lambda i: device(i, y, z, core))
    along_y = (4, y, lambda i: device(x, i, z, core))
    barrier = pltpu.get_barrier_semaphore()
    near = [where(lax.rem(mine + d, 4)) for _, mine, where in (along_x, along_y) for d in (1, 3)]
    for target in near + [pair[2](1 - core)]:
        pl.semaphore_signal(
            barrier, inc=1, device_id=target, device_id_type=pl.DeviceIdType.MESH
        )

    def greet(d, carry):
        pl.semaphore_signal(
            barrier,
            inc=1,
            device_id=column[2](lax.rem(z + d, 16)),
            device_id_type=pl.DeviceIdType.MESH,
        )
        return carry

    lax.fori_loop(1, 16, greet, 0)
    pl.semaphore_wait(barrier, 20)

    def lanes(i):
        return pl.ds(pl.multiple_of(i * 384, 128), 384)

    def rows(i):
        return pl.ds(lax.rem(i, 2) * 3, 3)

    def span(first, half):
        return pl.ds(first, 8) if half is None else pl.ds(first + 4 * half, 4)

    def first_x(i, half=None):
        return out.at[span(0, half), y // 2, core, rows(y), :, lanes(i)]

    def first_y(i, half=None):
        return out.at[span(0, half), i // 2, core, rows(i)]

    def second_y(i, half=None):
        return out.at[span(8, half), i // 2, core, rows(i), :, lanes(x)]

    def second_x(i, half=None):
        return out.at[span(8, half), :, core, :, :, lanes(i)]

    def remote(block, sems, number, target):
        return pltpu.make_async_remote_copy(
            src_ref=block,
            dst_ref=block,
            send_sem=sems.at[0, number],
            recv_sem=sems.at[1, number],
            device_id=target,
            device_id_type=pl.DeviceIdType.MESH,
        )

    def piece(i):
        return out.at[i, y // 2, core, rows(y), :, lanes(x)]

    own = pltpu.make_async_copy(x_ref.at[rows(y), :, lanes(x)], piece(z), own_sem)
    own.start()

    def send(d, carry):
        pltpu.make_async_remote_copy(
            src_ref=x_ref.at[rows(y), :, lanes(x)],
            dst_ref=piece(z),
            send_sem=column_sems.at[0, d],
            recv_sem=column_sems.at[1, z],
            device_id=column[2](lax.rem(z + d, 16)),
            device_id_type=pl.DeviceIdType.MESH,
        ).start()
        return carry

    def take(d, carry):
        peer = lax.rem(z + d, 16)
        copy = pltpu.make_async_remote_copy(
            src_ref=x_ref.at[rows(y), :, lanes(x)],
            dst_ref=piece(peer),
            send_sem=column_sems.at[0, d],
            recv_sem=column_sems.at[1, peer],
            device_id=column[2](peer),
            device_id_type=pl.DeviceIdType.MESH,
        )
        copy.wait_send()
        copy.wait_recv()
        return carry

    lax.fori_loop(1, 16, send, 0)
    own.wait()
    lax.fori_loop(1, 16, take, 0)

    def ring(group, block, base, share=None):
        _, mine, where = group
        right, left, far = (lax.rem(mine + d, 4) for d in (1, 3, 2))
        to_right, to_left = where(right), where(left)
        sends = [
            remote(block(mine), ring_sems, base, to_right),
            remote(block(mine), ring_sems, base + 1, to_left),
            remote(block(left, 0), ring_sems, base + 2, to_right),
            remote(block(right, 1), ring_sems, base + 3, to_left),
        ]
        arrivals = [block(left), block(right), block(far, 0), block(far, 1)]
        shared = []

        def arrive(i):
            remote(arrivals[i], ring_sems, base + i, to_left).wait_recv()
            if share is not None:
                give(arrivals[i], share + 1 + i)

        def give(part, number):
            copy = remote(part, core_sems, number, pair[2](1 - core))
            copy.start()
            shared.append(copy)

        def begin():
            sends[0].start()
            sends[1].start()
            if share is not None:
                give(block(mine), share)

        def middle():
            arrive(0)
            sends[2].start()
            arrive(1)
            sends[3].start()

        def end():
            arrive(2)
            arrive(3)

        def drain():
            for copy in sends + shared:
                copy.wait_send()

        return begin, middle, end, drain

    drains = []
    for pass_rings in (
        (ring(along_x, first_x, 0), ring(along_y, second_y, 4)),
        (ring(along_y, first_y, 8, 0), ring(along_x, second_x, 12, 5)),
    ):
        for step in range(3):
            for parts in pass_rings:
                parts[step]()
        drains += [parts[3] for parts in pass_rings]
    for drain in drains:
        drain()
    other = 1 - core

    def theirs_y(i, half=None):
        return out.at[span(0, half), i // 2, other, rows(i)]

    def theirs_x(i, half=None):
        return out.at[span(8, half), :, other, :, :, lanes(i)]

    for block, mine, base in ((theirs_y, y, 0), (theirs_x, x, 5)):
        right, left, far = (lax.rem(mine + d, 4) for d in (1, 3, 2))
        parts = [block(mine), block(left), block(right), block(far, 0), block(far, 1)]
        for i, part in enumerate(parts):
            remote(part, core_sems, base + i, pair[2](other)).wait_recv()


def gather(weight, number):
    shards = weight.shape[0] // 8
    out = pl.pallas_call(
        gather_kernel,
        out_shape=jax.ShapeDtypeStruct((16, 2, 2, shards, 8, weight.shape[1]), weight.dtype),
        in_specs=[pl.BlockSpec(memory_space=pltpu.VMEM)],
        out_specs=pl.BlockSpec(memory_space=pl.ANY),
        scratch_shapes=[
            pltpu.SemaphoreType.DMA((2, 16)),
            pltpu.SemaphoreType.DMA((2, 16)),
            pltpu.SemaphoreType.DMA((2, 10)),
            pltpu.SemaphoreType.DMA,
        ],
        compiler_params=pltpu.CompilerParams(collective_id=number, has_side_effects=True),
    )(weight.reshape(shards, 8, -1))
    return out.reshape(-1, weight.shape[1])


def on_device(features, start_noise, cotangent, in_weight, kernel, bn_gain, bn_shift, ends):
    frame_rows = features.shape[1]
    model_width = features.shape[2]
    tap_count = kernel.shape[0]
    shard_index = lax.axis_index("tm")
    group_index = lax.axis_index("dp")
    utter_end = lax.dynamic_index_in_dim(ends, group_index, 0, keepdims=False)
    live_count = jnp.sum(ends).astype(jnp.float32)
    utter_length = utter_end.astype(jnp.float32)
    frame_ids = shard_index * frame_rows + jnp.arange(frame_rows, dtype=jnp.int32)
    live = (frame_ids < utter_end).astype(jnp.float32)[:, None]
    weight_full = gather(in_weight, 7)
    inputs = features[0].astype(jnp.float32)
    perturbation = noise_scale * start_noise[0].astype(jnp.float32) * live
    upstream = live * cotangent[0].astype(jnp.float32) / ASCENT
    sizes = group_sizes(ends, frame_rows)
    counts = jnp.stack([1.0 / jnp.maximum(jnp.sum(live), 1.0), live_count])
    kernel_part = 0.0
    norm_part = 0.0
    for ascent_step in range(ASCENT):
        summed = inputs + perturbation
        normed, inverse = normalize(summed)
        hidden = lax.dot_general(
            normed.astype(jnp.bfloat16),
            weight_full,
            (((1,), (1,)), ((), ())),
            preferred_element_type=jnp.float32,
        )
        value_half = hidden[:, :model_width]
        gate_half = jax.nn.sigmoid(hidden[:, model_width:])
        glu = (value_half * gate_half * live).astype(jnp.bfloat16)
        back = ascent_step + 1 < ASCENT
        both, taps, *rest = conv_step(
            sizes, counts, glu, upstream, live, kernel, bn_gain, bn_shift, back, 1 + ascent_step
        )
        norm_part = norm_part + both
        kernel_part = kernel_part + taps
        if back:
            grad_glu = rest[0]
            grad_float = grad_glu.astype(jnp.float32)
            grad_hidden = jnp.concatenate(
                [grad_float * gate_half, grad_float * value_half * gate_half * (1.0 - gate_half)],
                axis=1,
            ).astype(jnp.bfloat16)
            grad_normed = jnp.dot(grad_hidden, weight_full, preferred_element_type=jnp.float32)
            direction = (
                live
                * inverse
                * (
                    grad_normed
                    - jnp.mean(grad_normed, axis=-1, keepdims=True)
                    - normed * jnp.mean(grad_normed * normed, axis=-1, keepdims=True)
                )
            )
            squares = jnp.sum((direction * direction).reshape(128, 12, 128), axis=(0, 1))[None]
            square_total = jnp.sum(square_sum(squares, 5))
            perturbation = perturbation + direction * (
                ascent_rate
                * jnp.sqrt(utter_length * model_width)
                / (jnp.sqrt(square_total) + ascent_epsilon)
            )
    width = model_width // lax.axis_size("tm")
    by_shard = kernel_part[:tap_count].reshape(tap_count, 16, 2, 2, width).transpose(3, 1, 2, 0, 4)
    by_shard = by_shard.reshape(64, tap_count * width)
    by_shard = jnp.pad(by_shard, ((0, 0), (0, 1024 - tap_count * width)))
    kernel_total = scatter_taps(by_shard.reshape(2, 16, 2, 8, 128), 6).reshape(-1)
    kernel_total = kernel_total[: tap_count * width].reshape(tap_count, width)
    norm_total = lax.dynamic_slice_in_dim(norm_part, shard_index * width, width, 1)
    return (perturbation[None], kernel_total, norm_total)


def solution(mesh):
    return jax.shard_map(
        on_device,
        mesh=mesh,
        in_specs=(
            P("dp", "tm", None),
            P("dp", "tm", None),
            P("dp", "tm", None),
            P("tm", None),
            P(),
            P(),
            P(),
            P(),
        ),
        out_specs=(P("dp", "tm", None), P(None, "tm"), P(None, "tm")),
        check_vma=False,
    )
```

```python
import jax
import jax.numpy as jnp
from jax import lax
from jax.experimental import pallas as pl
from jax.experimental.pallas import tpu as pltpu
from jax.sharding import PartitionSpec as P

ASCENT = 2

noise_scale = 0.5
ascent_rate = 0.5
layer_epsilon = 1e-05
batch_epsilon = 1e-05
ascent_epsilon = 1e-06


def normalize(summed):
    centre = summed - jnp.mean(summed, axis=-1, keepdims=True)
    inverse = lax.rsqrt(jnp.mean(centre * centre, axis=-1, keepdims=True) + layer_epsilon)
    return (centre * inverse, inverse)


def place():
    dp, tm = lax.axis_index("dp"), lax.axis_index("tm")
    x, y_lo = dp // 2, lax.rem(dp, 2)
    core, y_hi, z = lax.rem(tm, 2), lax.rem(tm // 2, 2), tm // 4
    return x, y_hi * 2 + y_lo, z, core


def device(x, y, z, core):
    return (x * 2 + lax.rem(y, 2), (z * 2 + y // 2) * 2 + core)


def groups():
    x, y, z, core = place()
    pair = (2, core, lambda i: device(x, y, z, i))
    plane = (16, x * 4 + y, lambda i: device(i // 4, lax.rem(i, 4), z, core))
    column = (16, z, lambda i: device(x, y, i, core))
    quad = (4, (y // 2) * 2 + core, lambda i: device(x, (i // 2) * 2 + lax.rem(y, 2), z, lax.rem(i, 2)))
    return pair, plane, column, quad


def meet(*members):
    barrier = pltpu.get_barrier_semaphore()
    for count, mine, where in members:

        def greet(d, carry):
            pl.semaphore_signal(
                barrier,
                inc=1,
                device_id=where(lax.rem(mine + d, count)),
                device_id_type=pl.DeviceIdType.MESH,
            )
            return carry

        lax.fori_loop(1, count, greet, 0)
    pl.semaphore_wait(barrier, sum(count - 1 for count, _, _ in members))


def exchange(group, source, landing, sems):
    count, mine, where = group

    def copy(d, out):
        peer = lax.rem(mine + d, count)
        slot = mine if out else peer
        return pltpu.make_async_remote_copy(
            src_ref=source(peer),
            dst_ref=landing.at[slot],
            send_sem=sems.at[0, d],
            recv_sem=sems.at[1, slot],
            device_id=where(peer),
            device_id_type=pl.DeviceIdType.MESH,
        )

    def start(d, carry):
        copy(d, True).start()
        return carry

    def finish(d, carry):
        copy(d, False).wait_send()
        copy(d, False).wait_recv()
        return carry

    lax.fori_loop(1, count, start, 0)
    lax.fori_loop(1, count, finish, 0)


def add_up(parts, count):
    total = parts[0]
    for i in range(1, count):
        total = total + parts[i]
    return total


def join_moments(parts, count, sizes, stage):
    half = parts.shape[1] // 2
    total = parts[0, :half]
    spread = parts[0, half:]
    for i in range(1, count):
        total = total + parts[i, :half]
        spread = spread + parts[i, half:]
    mean = total * sizes[stage, 2, 0]
    for i in range(count):
        apart = parts[i, :half] - sizes[stage, 0, i] * mean
        spread = spread + apart * apart * sizes[stage, 1, i]
    return jnp.concatenate([total, spread], axis=0)


def flat_plane():
    x, y, z, core = place()
    return (
        32,
        (x * 4 + y) * 2 + core,
        lambda i: device(i // 8, lax.rem(i // 2, 4), z, lax.rem(i, 2)),
    )


def sum_everywhere(owners, src, b1, b2, b3, sems, join):
    (count, me, where), column = flat_plane(), groups()[2]
    z = column[1]

    def copy(stage, source, landing, send, receive, peer):
        return pltpu.make_async_remote_copy(
            src_ref=source,
            dst_ref=landing,
            send_sem=sems.at[stage, 0, send],
            recv_sem=sems.at[stage, 1, receive],
            device_id=where(peer),
            device_id_type=pl.DeviceIdType.MESH,
        )

    def for_owners(body):
        def step(i, carry):
            @pl.when(i != me)
            def _():
                body(i)

            return carry

        lax.fori_loop(0, owners, step, 0)

    def for_peers(body):
        def step(d, carry):
            body(d, lax.rem(me + d, count))
            return carry

        lax.fori_loop(1, count, step, 0)

    for_owners(lambda i: copy(0, src.at[i], b1.at[me], i, me, i).start())

    @pl.when(me < owners)
    def _():
        b1[me] = src[me]
        for_peers(lambda d, peer: copy(0, src.at[0], b1.at[peer], 0, peer, peer).wait_recv())
        b2[z] = join(b1, 32, 0)
        exchange(column, lambda peer: b2.at[z], b2, sems.at[1])
        b3[me] = join(b2, 16, 1)
        for_peers(lambda d, peer: copy(2, b3.at[me], b3.at[me], d, me, peer).start())
        for_peers(lambda d, peer: copy(2, b3.at[me], b3.at[me], d, me, peer).wait_send())

    for_owners(lambda i: copy(0, src.at[i], b1.at[me], i, me, i).wait_send())
    for_owners(lambda i: copy(2, b3.at[i], b3.at[i], 0, i, i).wait_recv())


def neighbours():
    dp, tm = lax.axis_index("dp"), lax.axis_index("tm")
    return (3, 0, lambda i: (dp, lax.rem(tm + 1 + (i - 1) * 62, 64)))


def conv_kernel(
    back, sizes, counts, glu_ref, up_ref, live_ref, kernel_ref, gain_ref, shift_ref,
    both_ref, taps_ref, grad_glu_ref,
    padded, conv_ref, scaled_ref, pre_ref, inv_ref, grad_ref, halo1, halo2,
    s1, a1, a2, a3, s2, c1, c2, c3, sems1, sems2, halo_sems,
):
    meet(flat_plane(), groups()[2], neighbours())
    tm = lax.axis_index("tm")
    rows, width = glu_ref.shape
    total_live = counts[1]
    beside = neighbours()[2]

    def at(i):
        return pl.ds(pl.multiple_of(i * 128, 128), 128)

    def each(body):
        def step(i, carry):
            body(i)
            return carry

        lax.fori_loop(0, width // 128, step, 0)

    def halo_copies(block, halo, base):
        return [
            pltpu.make_async_remote_copy(
                src_ref=block.at[pl.ds((rows - 16) * (1 - side), 16)],
                dst_ref=halo.at[side],
                send_sem=halo_sems.at[0, base + side],
                recv_sem=halo_sems.at[1, base + side],
                device_id=beside(1 + side),
                device_id_type=pl.DeviceIdType.MESH,
            )
            for side in (0, 1)
        ]

    def fill(block, halo):
        first = jnp.where(tm > 0, 1.0, 0.0).astype(jnp.float32)
        last = jnp.where(tm < 63, 1.0, 0.0).astype(jnp.float32)

        def tile(i):
            padded[pl.ds(0, 16), at(i)] = halo[0, :, at(i)].astype(jnp.float32) * first
            padded[pl.ds(16, rows), at(i)] = block[:, at(i)].astype(jnp.float32)
            padded[pl.ds(rows + 16, 16), at(i)] = halo[1, :, at(i)].astype(jnp.float32) * last

        each(tile)

    def convolve(i, start_of):
        total = None
        for j in range(31):
            term = kernel_ref[pl.ds(j, 1), at(i)] * padded[pl.ds(start_of(j), rows), at(i)]
            total = term if total is None else total + term
        return total

    first_halo = halo_copies(glu_ref, halo1, 0)
    for copy in first_halo:
        copy.start()
    for copy in first_halo:
        copy.wait()
    fill(glu_ref, halo1)

    def moments(i):
        part, live = convolve(i, lambda j: j + 1), live_ref[...]
        conv_ref[:, at(i)] = part
        local = jnp.sum(part * live, axis=0, keepdims=True)
        apart = part - local * counts[0]
        s1[i, 0:1] = local
        s1[i, 1:2] = jnp.sum(live * apart * apart, axis=0, keepdims=True)

    each(moments)
    sum_everywhere(width // 128, s1, a1, a2, a3, sems1, lambda p, n, k: join_moments(p, n, sizes, k))

    def activate(i):
        found = a3[i]
        inv_std = lax.rsqrt(found[1:2] / total_live + batch_epsilon)
        scaled = (conv_ref[:, at(i)] - found[0:1] / total_live) * inv_std
        pre_act = gain_ref[:, at(i)] * scaled + shift_ref[:, at(i)]
        pre_sigmoid = jax.nn.sigmoid(pre_act)
        grad_pre = up_ref[:, at(i)] * pre_sigmoid * (1.0 + pre_act * (1.0 - pre_sigmoid))
        scaled_ref[:, at(i)] = scaled
        pre_ref[:, at(i)] = grad_pre
        inv_ref[:, at(i)] = inv_std
        s2[i, 0:1] = jnp.sum(grad_pre * scaled, axis=0, keepdims=True)
        s2[i, 1:2] = jnp.sum(grad_pre, axis=0, keepdims=True)

    each(activate)
    sum_everywhere(width // 128, s2, c1, c2, c3, sems2, lambda p, n, k: add_up(p, n))

    def backward(i):
        found = c3[i]
        both_ref[:, at(i)] = found
        scaled, grad_pre = scaled_ref[:, at(i)], pre_ref[:, at(i)]
        grad = (
            live_ref[...]
            * (inv_ref[:, at(i)] * gain_ref[:, at(i)])
            * (grad_pre - (found[1:2] + scaled * found[0:1]) / total_live)
        )
        grad_ref[:, at(i)] = grad.astype(jnp.bfloat16)

    each(backward)
    if back:
        second_halo = halo_copies(grad_ref, halo2, 2)
        for copy in second_halo:
            copy.start()

    def tap_sums(i):
        grad = grad_ref[:, at(i)].astype(jnp.float32)
        for j in range(31):
            window = padded[pl.ds(j + 1, rows), at(i)]
            taps_ref[pl.ds(j, 1), at(i)] = jnp.sum(grad * window, axis=0, keepdims=True)
        taps_ref[pl.ds(31, 1), at(i)] = jnp.zeros((1, 128), jnp.float32)

    each(tap_sums)
    if back:
        for copy in second_halo:
            copy.wait()
        fill(grad_ref, halo2)

        def input_grad(i):
            part = convolve(i, lambda j: 31 - j) * live_ref[...]
            grad_glu_ref[:, at(i)] = part.astype(jnp.bfloat16)

        each(input_grad)


def conv_step(sizes, counts, glu, upstream, live, kernel, gain, shift, back, number):
    rows, width = glu.shape
    smem, vmem = pl.BlockSpec(memory_space=pltpu.SMEM), pl.BlockSpec(memory_space=pltpu.VMEM)
    slots = [pltpu.VMEM((n, 2, 128), jnp.float32) for n in (32, 32, 16, 32)]
    whole = pltpu.VMEM((rows, width), jnp.float32)
    halo = pltpu.VMEM((2, 16, width), jnp.bfloat16)
    shapes = [
        jax.ShapeDtypeStruct((2, width), jnp.float32),
        jax.ShapeDtypeStruct((32, width), jnp.float32),
    ]
    if back:
        shapes.append(jax.ShapeDtypeStruct((rows, width), jnp.bfloat16))

    def body(*refs):
        refs = list(refs) if back else list(refs[:10]) + [None] + list(refs[10:])
        conv_kernel(back, *refs)

    return pl.pallas_call(
        body,
        out_shape=shapes,
        in_specs=[smem, smem] + [vmem] * 6,
        out_specs=[vmem] * len(shapes),
        scratch_shapes=[
            pltpu.VMEM((rows + 32, width), jnp.float32),
            whole,
            whole,
            whole,
            pltpu.VMEM((1, width), jnp.float32),
            pltpu.VMEM((rows, width), jnp.bfloat16),
            halo,
            halo,
        ]
        + slots
        + slots
        + [pltpu.SemaphoreType.DMA((3, 2, 32)), pltpu.SemaphoreType.DMA((3, 2, 32))]
        + [pltpu.SemaphoreType.DMA((2, 4))],
        compiler_params=pltpu.CompilerParams(collective_id=number, has_side_effects=True),
    )(sizes, counts, glu, upstream, jnp.broadcast_to(live, (rows, 128)),
      kernel, gain[None], shift[None])


def group_sizes(ends, frame_rows):
    _, _, z, _ = place()
    starts = frame_rows * jnp.arange(64, dtype=jnp.int32)
    live = jnp.clip(ends[:, None] - starts[None, :], 0, frame_rows).astype(jnp.float32)
    live = live.reshape(4, 2, 16, 2, 2).transpose(2, 0, 3, 1, 4).reshape(16, 32)
    here = lax.dynamic_index_in_dim(live, z, 0, keepdims=False)
    sizes = jnp.stack([here, jnp.pad(jnp.sum(live, axis=1), (0, 16))])
    each = jnp.where(sizes > 0, 1.0 / jnp.maximum(sizes, 1.0), 0.0)
    whole = jnp.sum(sizes, axis=1, keepdims=True)
    whole = jnp.broadcast_to(1.0 / jnp.maximum(whole, 1.0), sizes.shape)
    return jnp.stack([sizes, each, whole], axis=1)


def square_sum_kernel(x_ref, out_ref, b0, b1, sems):
    _, _, column, quad = groups()
    meet(column, quad)
    b0[column[1]] = x_ref[...]
    exchange(column, lambda peer: b0.at[column[1]], b0, sems.at[0])
    b1[quad[1]] = add_up(b0, 16)
    exchange(quad, lambda peer: b1.at[quad[1]], b1, sems.at[1])
    out_ref[...] = add_up(b1, 4)


def square_sum(rows, number):
    return pl.pallas_call(
        square_sum_kernel,
        out_shape=jax.ShapeDtypeStruct((1, 128), jnp.float32),
        in_specs=[pl.BlockSpec(memory_space=pltpu.VMEM)],
        out_specs=pl.BlockSpec(memory_space=pltpu.VMEM),
        scratch_shapes=[
            pltpu.VMEM((16, 1, 128), jnp.float32),
            pltpu.VMEM((4, 1, 128), jnp.float32),
            pltpu.SemaphoreType.DMA((2, 2, 16)),
        ],
        compiler_params=pltpu.CompilerParams(collective_id=number, has_side_effects=True),
    )(rows)


def scatter_taps_kernel(x_ref, out_ref, b0, b1, b2, s1, s2, sems):
    pair, plane, column, _ = groups()
    x, y, z, core = place()
    meet(pair, plane, column)
    exchange(pair, lambda peer: x_ref.at[peer], b0, sems.at[0])
    s1[...] = x_ref[core] + b0[1 - core]
    b1[z] = s1[z]
    exchange(column, lambda peer: s1.at[peer], b1, sems.at[1])
    s2[...] = add_up(b1, 16)
    b2[plane[1]] = s2[y // 2]
    exchange(plane, lambda peer: s2.at[lax.rem(peer, 4) // 2], b2, sems.at[2])
    out_ref[...] = add_up(b2, 16)


def scatter_taps(taps, number):
    return pl.pallas_call(
        scatter_taps_kernel,
        out_shape=jax.ShapeDtypeStruct((8, 128), jnp.float32),
        in_specs=[pl.BlockSpec(memory_space=pltpu.VMEM)],
        out_specs=pl.BlockSpec(memory_space=pltpu.VMEM),
        scratch_shapes=[
            pltpu.VMEM((2, 16, 2, 8, 128), jnp.float32),
            pltpu.VMEM((16, 2, 8, 128), jnp.float32),
            pltpu.VMEM((16, 8, 128), jnp.float32),
            pltpu.VMEM((16, 2, 8, 128), jnp.float32),
            pltpu.VMEM((2, 8, 128), jnp.float32),
            pltpu.SemaphoreType.DMA((3, 2, 16)),
        ],
        compiler_params=pltpu.CompilerParams(collective_id=number, has_side_effects=True),
    )(taps)


def gather_kernel(x_ref, out, column_sems, ring_sems, core_sems, own_sem):
    x, y, z, core = place()
    pair, _, column, _ = groups()
    along_x = (4, x, lambda i: device(i, y, z, core))
    along_y = (4, y, lambda i: device(x, i, z, core))
    barrier = pltpu.get_barrier_semaphore()
    near = [where(lax.rem(mine + d, 4)) for _, mine, where in (along_x, along_y) for d in (1, 3)]
    for target in near + [pair[2](1 - core)]:
        pl.semaphore_signal(
            barrier, inc=1, device_id=target, device_id_type=pl.DeviceIdType.MESH
        )

    def greet(d, carry):
        pl.semaphore_signal(
            barrier,
            inc=1,
            device_id=column[2](lax.rem(z + d, 16)),
            device_id_type=pl.DeviceIdType.MESH,
        )
        return carry

    lax.fori_loop(1, 16, greet, 0)
    pl.semaphore_wait(barrier, 20)

    def lanes(i):
        return pl.ds(pl.multiple_of(i * 384, 128), 384)

    def rows(i):
        return pl.ds(lax.rem(i, 2) * 3, 3)

    def span(first, half):
        return pl.ds(first, 8) if half is None else pl.ds(first + 4 * half, 4)

    def first_x(i, half=None):
        return out.at[span(0, half), y // 2, core, rows(y), :, lanes(i)]

    def first_y(i, half=None):
        return out.at[span(0, half), i // 2, core, rows(i)]

    def second_y(i, half=None):
        return out.at[span(8, half), i // 2, core, rows(i), :, lanes(x)]

    def second_x(i, half=None):
        return out.at[span(8, half), :, core, :, :, lanes(i)]

    def remote(block, sems, number, target):
        return pltpu.make_async_remote_copy(
            src_ref=block,
            dst_ref=block,
            send_sem=sems.at[0, number],
            recv_sem=sems.at[1, number],
            device_id=target,
            device_id_type=pl.DeviceIdType.MESH,
        )

    def piece(i):
        return out.at[i, y // 2, core, rows(y), :, lanes(x)]

    own = pltpu.make_async_copy(x_ref.at[rows(y), :, lanes(x)], piece(z), own_sem)
    own.start()

    def send(d, carry):
        pltpu.make_async_remote_copy(
            src_ref=x_ref.at[rows(y), :, lanes(x)],
            dst_ref=piece(z),
            send_sem=column_sems.at[0, d],
            recv_sem=column_sems.at[1, z],
            device_id=column[2](lax.rem(z + d, 16)),
            device_id_type=pl.DeviceIdType.MESH,
        ).start()
        return carry

    def take(d, carry):
        peer = lax.rem(z + d, 16)
        copy = pltpu.make_async_remote_copy(
            src_ref=x_ref.at[rows(y), :, lanes(x)],
            dst_ref=piece(peer),
            send_sem=column_sems.at[0, d],
            recv_sem=column_sems.at[1, peer],
            device_id=column[2](peer),
            device_id_type=pl.DeviceIdType.MESH,
        )
        copy.wait_send()
        copy.wait_recv()
        return carry

    lax.fori_loop(1, 16, send, 0)
    own.wait()
    lax.fori_loop(1, 16, take, 0)

    def ring(group, block, base, share=None):
        _, mine, where = group
        right, left, far = (lax.rem(mine + d, 4) for d in (1, 3, 2))
        to_right, to_left = where(right), where(left)
        sends = [
            remote(block(mine), ring_sems, base, to_right),
            remote(block(mine), ring_sems, base + 1, to_left),
            remote(block(left, 0), ring_sems, base + 2, to_right),
            remote(block(right, 1), ring_sems, base + 3, to_left),
        ]
        arrivals = [block(left), block(right), block(far, 0), block(far, 1)]
        shared = []

        def arrive(i):
            remote(arrivals[i], ring_sems, base + i, to_left).wait_recv()
            if share is not None:
                give(arrivals[i], share + 1 + i)

        def give(part, number):
            copy = remote(part, core_sems, number, pair[2](1 - core))
            copy.start()
            shared.append(copy)

        def begin():
            sends[0].start()
            sends[1].start()
            if share is not None:
                give(block(mine), share)

        def middle():
            arrive(0)
            sends[2].start()
            arrive(1)
            sends[3].start()

        def end():
            arrive(2)
            arrive(3)

        def drain():
            for copy in sends + shared:
                copy.wait_send()

        return begin, middle, end, drain

    drains = []
    for pass_rings in (
        (ring(along_x, first_x, 0), ring(along_y, second_y, 4)),
        (ring(along_y, first_y, 8, 0), ring(along_x, second_x, 12, 5)),
    ):
        for step in range(3):
            for parts in pass_rings:
                parts[step]()
        drains += [parts[3] for parts in pass_rings]
    for drain in drains:
        drain()
    other = 1 - core

    def theirs_y(i, half=None):
        return out.at[span(0, half), i // 2, other, rows(i)]

    def theirs_x(i, half=None):
        return out.at[span(8, half), :, other, :, :, lanes(i)]

    for block, mine, base in ((theirs_y, y, 0), (theirs_x, x, 5)):
        right, left, far = (lax.rem(mine + d, 4) for d in (1, 3, 2))
        parts = [block(mine), block(left), block(right), block(far, 0), block(far, 1)]
        for i, part in enumerate(parts):
            remote(part, core_sems, base + i, pair[2](other)).wait_recv()


def gather(weight, number):
    shards = weight.shape[0] // 8
    out = pl.pallas_call(
        gather_kernel,
        out_shape=jax.ShapeDtypeStruct((16, 2, 2, shards, 8, weight.shape[1]), weight.dtype),
        in_specs=[pl.BlockSpec(memory_space=pltpu.VMEM)],
        out_specs=pl.BlockSpec(memory_space=pl.ANY),
        scratch_shapes=[
            pltpu.SemaphoreType.DMA((2, 16)),
            pltpu.SemaphoreType.DMA((2, 16)),
            pltpu.SemaphoreType.DMA((2, 10)),
            pltpu.SemaphoreType.DMA,
        ],
        compiler_params=pltpu.CompilerParams(collective_id=number, has_side_effects=True),
    )(weight.reshape(shards, 8, -1))
    return out.reshape(-1, weight.shape[1])


def on_device(features, start_noise, cotangent, in_weight, kernel, bn_gain, bn_shift, ends):
    frame_rows = features.shape[1]
    model_width = features.shape[2]
    tap_count = kernel.shape[0]
    shard_index = lax.axis_index("tm")
    group_index = lax.axis_index("dp")
    utter_end = lax.dynamic_index_in_dim(ends, group_index, 0, keepdims=False)
    live_count = jnp.sum(ends).astype(jnp.float32)
    utter_length = utter_end.astype(jnp.float32)
    frame_ids = shard_index * frame_rows + jnp.arange(frame_rows, dtype=jnp.int32)
    live = (frame_ids < utter_end).astype(jnp.float32)[:, None]
    weight_full = gather(in_weight, 7)
    inputs = features[0].astype(jnp.float32)
    perturbation = noise_scale * start_noise[0].astype(jnp.float32) * live
    upstream = live * cotangent[0].astype(jnp.float32) / ASCENT
    sizes = group_sizes(ends, frame_rows)
    counts = jnp.stack([1.0 / jnp.maximum(jnp.sum(live), 1.0), live_count])
    kernel_part = 0.0
    norm_part = 0.0
    for ascent_step in range(ASCENT):
        summed = inputs + perturbation
        normed, inverse = normalize(summed)
        hidden = lax.dot_general(
            normed.astype(jnp.bfloat16),
            weight_full,
            (((1,), (1,)), ((), ())),
            preferred_element_type=jnp.float32,
        )
        value_half = hidden[:, :model_width]
        gate_half = jax.nn.sigmoid(hidden[:, model_width:])
        glu = (value_half * gate_half * live).astype(jnp.bfloat16)
        back = ascent_step + 1 < ASCENT
        both, taps, *rest = conv_step(
            sizes, counts, glu, upstream, live, kernel, bn_gain, bn_shift, back, 1 + ascent_step
        )
        norm_part = norm_part + both
        kernel_part = kernel_part + taps
        if back:
            grad_glu = rest[0]
            grad_float = grad_glu.astype(jnp.float32)
            grad_hidden = jnp.concatenate(
                [grad_float * gate_half, grad_float * value_half * gate_half * (1.0 - gate_half)],
                axis=1,
            ).astype(jnp.bfloat16)
            grad_normed = jnp.dot(grad_hidden, weight_full, preferred_element_type=jnp.float32)
            direction = (
                live
                * inverse
                * (
                    grad_normed
                    - jnp.mean(grad_normed, axis=-1, keepdims=True)
                    - normed * jnp.mean(grad_normed * normed, axis=-1, keepdims=True)
                )
            )
            squares = jnp.sum((direction * direction).reshape(128, 12, 128), axis=(0, 1))[None]
            square_total = jnp.sum(square_sum(squares, 5))
            perturbation = perturbation + direction * (
                ascent_rate
                * jnp.sqrt(utter_length * model_width)
                / (jnp.sqrt(square_total) + ascent_epsilon)
            )
    width = model_width // lax.axis_size("tm")
    by_shard = kernel_part[:tap_count].reshape(tap_count, 16, 2, 2, width).transpose(3, 1, 2, 0, 4)
    by_shard = by_shard.reshape(64, tap_count * width)
    by_shard = jnp.pad(by_shard, ((0, 0), (0, 1024 - tap_count * width)))
    kernel_total = scatter_taps(by_shard.reshape(2, 16, 2, 8, 128), 6).reshape(-1)
    kernel_total = kernel_total[: tap_count * width].reshape(tap_count, width)
    norm_total = lax.dynamic_slice_in_dim(norm_part, shard_index * width, width, 1)
    return (perturbation[None], kernel_total, norm_total)


def solution(mesh):
    return jax.shard_map(
        on_device,
        mesh=mesh,
        in_specs=(
            P("dp", "tm", None),
            P("dp", "tm", None),
            P("dp", "tm", None),
            P("tm", None),
            P(),
            P(),
            P(),
            P(),
        ),
        out_specs=(P("dp", "tm", None), P(None, "tm"), P(None, "tm")),
        check_vma=False,
    )
```
